32 devices in a mesh: fsdp: 2 (over x), ctx: 4 (over z), tp: 4 (over y, core).
Axes of the slice: x: 2, y: 2, z: 4, core: 2. Of those that a mesh axis runs over, the one named last changes fastest.
Arguments:
- tokens: bfloat16 [4, 2048, 2048], P('fsdp', 'ctx'), may hold values from -6 to 6
- tree_position: int32 [4, 2048], P('fsdp', 'ctx'), may hold values from 0 to 2047, as said below
- segment: int32 [4, 2048], P('fsdp', 'ctx'), may hold values from 0 to 6, as said below
- parent_table: int32 [4, 7], P('fsdp'), may hold values from 0 to 2, as said below
- norm1_gain: float32 [2048], replicated, may hold values from 0.5 to 1.5
- norm1_shift: float32 [2048], replicated, may hold values from -4 to 4
- query_weight: bfloat16 [2048, 2048], P('fsdp', 'tp'), may hold values from -0.125 to 0.125
- query_bias: float32 [2048], P('tp'), may hold values from -4 to 4
- key_weight: bfloat16 [2048, 2048], P('fsdp', 'tp'), may hold values from -0.125 to 0.125
- value_weight: bfloat16 [2048, 2048], P('fsdp', 'tp'), may hold values from -0.125 to 0.125
- value_bias: float32 [2048], P('tp'), may hold values from -0.75 to 0.75
- out_weight: bfloat16 [2048, 2048], P('tp', 'fsdp'), may hold values from -1.5 to 1.5
- out_bias: float32 [2048], replicated, may hold values from -4 to 4
- norm2_gain: float32 [2048], replicated, may hold values from 0.5 to 1.5
- norm2_shift: float32 [2048], replicated, may hold values from -4 to 4
- up_weight: bfloat16 [2048, 8192], P('fsdp', 'tp'), may hold values from -0.125 to 0.125
- up_bias: float32 [8192], P('tp'), may hold values from -4 to 4
- down_weight: bfloat16 [8192, 2048], P('tp', 'fsdp'), may hold values from -0.0625 to 0.0625
- down_bias: float32 [2048], replicated, may hold values from -4 to 4
- cotangent: bfloat16 [4, 2048, 2048], P('fsdp', 'ctx'), may hold values from -6 to 6
Outputs:
- layer_out: bfloat16 [4, 2048, 2048], P('fsdp', 'ctx')
- grad_tokens: bfloat16 [4, 2048, 2048], P('fsdp', 'ctx')
- grad_norm1_gain: float32 [2048], P(('fsdp', 'ctx'))
- grad_norm1_shift: float32 [2048], P(('fsdp', 'ctx'))
- grad_query_weight: float32 [2048, 2048], P(('fsdp', 'ctx'), 'tp')
- grad_query_bias: float32 [2048], P('tp')
- grad_key_weight: float32 [2048, 2048], P(('fsdp', 'ctx'), 'tp')
- grad_value_weight: float32 [2048, 2048], P(('fsdp', 'ctx'), 'tp')
- grad_value_bias: float32 [2048], P('tp')
- grad_out_weight: float32 [2048, 2048], P('tp', ('fsdp', 'ctx'))
- grad_out_bias: float32 [2048], P(('fsdp', 'ctx'))
- grad_norm2_gain: float32 [2048], P(('fsdp', 'ctx'))
- grad_norm2_shift: float32 [2048], P(('fsdp', 'ctx'))
- grad_up_weight: float32 [2048, 8192], P(('fsdp', 'ctx'), 'tp')
- grad_up_bias: float32 [8192], P('tp')
- grad_down_weight: float32 [8192, 2048], P('tp', ('fsdp', 'ctx'))
- grad_down_bias: float32 [2048], P(('fsdp', 'ctx'))
The draws below stay inside these ranges and needn't reach their ends.
Inputs may be any that keep to these rules, and one draw needn't show every extreme that they name: `tree_position`: within each tree the rows hold the positions 0 to 2047 once each; every aligned run of 64 rows holds 64 consecutive positions in increasing order. `segment`: along increasing positions a tree runs through segments 0 to 6 in order, each nonempty and contiguous: the trunk 0 with 1024 positions, branches 1 and 2 with 512 together, leaves 3 to 6 with 512 together. `parent_table`: entry s of a tree's row is the parent of segment s: 0 for segments 0, 1 and 2; 1 for leaf 3; 2 for leaf 6; 1 or 2 for leaves 4 and 5.
All inputs are finite; a program needn't handle non-finite values.
Results may differ from the reference program's by a relative error of at most 0.024.
Values may be sent and summed in bfloat16 or wider, within the bound.
No kernel may reach another device: no remote copies, remote signals or barrier semaphores. Data moves between devices by JAX's collectives and lax.ppermute only.
A program may use at most 256 MiB of HBM per device.

```python
import math
import jax
import jax.numpy as jnp
from jax import lax

D = 2048
H = 16
HD = 128
FF = 8192
TRUNK = 1024
BRANCH = 256
LEAF = 128
LAYB = 64
TREE = 2048
TREES = 4
N_CTX = 4


def tree_layout(key):
    blocks = TREE // LAYB
    base_key = jax.random.fold_in(key, 11)

    def one_tree(tree_key):
        order = jax.random.permutation(jax.random.fold_in(tree_key, 1), blocks).astype(jnp.int32)
        rows = jnp.arange(TREE, dtype=jnp.int32)
        position = order[rows // LAYB] * LAYB + rows % LAYB
        branch_move = jax.random.randint(jax.random.fold_in(tree_key, 2), (1,), -(BRANCH // 2), BRANCH // 2 + 1).astype(jnp.int32)
        leaf_move = jax.random.randint(jax.random.fold_in(tree_key, 3), (2,), -(LEAF // 2), LEAF // 2 + 1).astype(jnp.int32)
        offsets = jnp.concatenate([jnp.zeros((1,), jnp.int32), branch_move, -branch_move, leaf_move[0:1], -leaf_move[0:1], leaf_move[1:2], -leaf_move[1:2]])
        lengths = jnp.array([TRUNK, BRANCH, BRANCH, LEAF, LEAF, LEAF, LEAF], dtype=jnp.int32) + offsets
        bounds = jnp.cumsum(lengths)[:-1]
        segs = jnp.sum((position[:, None] >= bounds[None, :]).astype(jnp.int32), axis=1)
        return (position, segs)
    tree_keys = jax.random.split(base_key, TREES)
    return jax.vmap(one_tree)(tree_keys)


def draw_tree_position(key, part):
    return tree_layout(key)[0]


def draw_segment(key, part):
    return tree_layout(key)[1]


def draw_parent_table(key, part):
    middle = jax.random.randint(jax.random.fold_in(key, 29), (TREES, 2), 1, 3).astype(jnp.int32)
    ones = jnp.ones((TREES, 1), jnp.int32)
    return jnp.concatenate([jnp.zeros((TREES, 3), jnp.int32), ones, middle, 2 * ones], axis=1)


def spiked(drawn, rng, source, target, blocks, factor):
    def block_of(dim):
        return (jnp.arange(drawn.shape[dim]) // (drawn.shape[dim] // blocks)).reshape((-1,) + (1,) * (drawn.ndim - 1 - dim))

    near = jax.random.permutation(rng, blocks)[block_of(target)]
    second = (block_of(target) + blocks // 2) % blocks
    return jnp.where((block_of(source) == near) | (block_of(source) == second), factor * drawn, drawn)


def steps_of(stream_key, shape, pieces, low, high):
    level = 1.0
    for axis_at, parts in pieces:
        draws = jax.random.uniform(jax.random.fold_in(jax.random.fold_in(stream_key, 6), axis_at), (parts,), jnp.float32, low / len(pieces), high / len(pieces))
        level = level * jnp.repeat(jnp.exp(draws), shape[axis_at] // parts).reshape((-1,) + (1,) * (len(shape) - 1 - axis_at))
    return level


def scatter_about(own_key, shape, scale, most, pieces=(), held_as=jnp.bfloat16):
    entries = scale * jax.random.normal(own_key, shape, jnp.float32)
    if pieces:
        entries = entries * steps_of(own_key, shape, pieces, -0.22, 0.18)
    return jnp.clip(entries, -most, most).astype(held_as)


def heavy_noise(stream_key, extent, width, bound, cuts, heavy, kind=jnp.bfloat16):
    entries = width * jax.random.normal(stream_key, extent, jnp.float32)
    if cuts:
        entries = entries * steps_of(stream_key, extent, cuts, -0.22, 0.18)
    return jnp.clip(spiked(entries, jax.random.fold_in(stream_key, 3), *heavy), -bound, bound).astype(kind)


def setup_inputs(seed: int = 0) -> dict:
    seeds = jax.random.split(jax.random.key(seed), 21)
    tokens = scatter_about(seeds[0], (TREES, TREE, D), 1.0, 6.0, ((0, 2), (1, 4)))
    tree_position = draw_tree_position(jax.random.fold_in(seeds[20], 71), 0)
    segment = draw_segment(jax.random.fold_in(seeds[20], 71), 0)
    parent_table = draw_parent_table(jax.random.fold_in(seeds[20], 71), 0)
    norm1_gain = jnp.clip(1.0 + 0.1 * jax.random.normal(seeds[4], (D,), jnp.float32), 0.5, 1.5)
    norm1_shift = scatter_about(seeds[5], (D,), 0.3, 4.0, (), jnp.float32)
    query_weight = scatter_about(seeds[6], (D, D), D ** -0.5, 0.125, ((0, 2), (1, 4)))
    query_bias = scatter_about(seeds[7], (D,), 0.3, 4.0, ((0, 4),), jnp.float32)
    key_weight = scatter_about(seeds[8], (D, D), D ** -0.5, 0.125, ((0, 2), (1, 4)))
    value_weight = scatter_about(seeds[9], (D, D), D ** -0.5, 0.125, ((0, 2), (1, 4)))
    value_bias = scatter_about(seeds[10], (D,), 0.05, 0.75, ((0, 4),), jnp.float32)
    out_weight = scatter_about(seeds[11], (D, D), (max(D // 128, 1)) ** -0.5, 1.5, ((0, 4), (1, 2)))
    out_bias = scatter_about(seeds[12], (D,), 0.3, 4.0, (), jnp.float32)
    norm2_gain = jnp.clip(1.0 + 0.1 * jax.random.normal(seeds[13], (D,), jnp.float32), 0.5, 1.5)
    norm2_shift = scatter_about(seeds[14], (D,), 0.3, 4.0, (), jnp.float32)
    up_weight = scatter_about(seeds[15], (D, FF), D ** -0.5, 0.125, ((0, 2), (1, 4)))
    up_bias = scatter_about(seeds[16], (FF,), 0.3, 4.0, ((0, 4),), jnp.float32)
    down_weight = scatter_about(seeds[17], (FF, D), FF ** -0.5, 0.0625, ((0, 4), (1, 2)))
    down_bias = scatter_about(seeds[18], (D,), 0.3, 4.0, (), jnp.float32)
    cotangent = heavy_noise(seeds[19], (TREES, TREE, D), 1.0, 6.0, ((0, 2), (1, 4)), (1, 2, 4, 2.0))
    return dict(tokens=tokens, tree_position=tree_position, segment=segment, parent_table=parent_table, norm1_gain=norm1_gain, norm1_shift=norm1_shift, query_weight=query_weight, query_bias=query_bias, key_weight=key_weight, value_weight=value_weight, value_bias=value_bias, out_weight=out_weight, out_bias=out_bias, norm2_gain=norm2_gain, norm2_shift=norm2_shift, up_weight=up_weight, up_bias=up_bias, down_weight=down_weight, down_bias=down_bias, cotangent=cotangent)


@jax.custom_vjp
def low(v):
    return lax.optimization_barrier(v.astype(jnp.bfloat16)).astype(jnp.float32)

@jax.custom_vjp
def low_back(v):
    return v

def low_keep(v):
    return (low(v), None)

def low_pass(kept, grad):
    return (grad,)

def back_keep(v):
    return (v, None)

def back_low(kept, grad):
    return (low(grad),)
low.defvjp(low_keep, low_pass)
low_back.defvjp(back_keep, back_low)
NEGATIVE = -1000000000.0

def dense(left, right):
    return jnp.dot(left, right, precision=lax.Precision.HIGHEST, preferred_element_type=jnp.float32)

def norm_rows(values, gain, shift):
    centre = lax.optimization_barrier(jnp.mean(values, axis=-1, keepdims=True))
    centred = values - centre
    spread = lax.optimization_barrier(jnp.mean(centred * centred, axis=-1, keepdims=True))
    return centred * lax.rsqrt(spread + 1e-05) * gain + shift

def on_path(query_pos, query_seg, key_pos, key_seg, parent):
    labels = jnp.arange(parent.shape[0], dtype=jnp.int32)
    first = lax.optimization_barrier(jnp.sum(jnp.where(query_seg[:, None] == labels[None, :], parent[None, :], 0), axis=1))
    second = lax.optimization_barrier(jnp.sum(jnp.where(first[:, None] == labels[None, :], parent[None, :], 0), axis=1))
    along = (key_seg[None, :] == query_seg[:, None]) | (key_seg[None, :] == first[:, None]) | (key_seg[None, :] == second[:, None])
    return along & (key_pos[None, :] <= query_pos[:, None])

def tree_forward(params, inputs, position, segs, parent):
    first_gain, first_shift, w_query, b_query, w_key, w_value, b_value, w_out, b_out, second_gain, second_shift, w_up, b_up, w_down, b_down = params
    normed = low(norm_rows(inputs, first_gain, first_shift))
    queries = low_back(low(dense(normed, w_query) + b_query))
    keys_all = low_back(low(dense(normed, w_key)))
    values_all = low_back(low(dense(normed, w_value) + b_value))
    key_heads = keys_all.reshape(TREE, H, HD)
    value_heads = values_all.reshape(TREE, H, HD)
    blocks = N_CTX
    block_rows = TREE // blocks
    score_scale = 1.0 / math.sqrt(HD)

    def attend(block_part):
        block_query, block_pos, block_seg = block_part
        scores = jnp.einsum('qhd,khd->hqk', block_query, key_heads, precision=lax.Precision.HIGHEST) * score_scale
        visible = on_path(block_pos, block_seg, position, segs, parent)
        scores = low_back(jnp.where(visible[None], scores, NEGATIVE))
        softmax_weights = jax.nn.softmax(scores, axis=-1)
        return jnp.einsum('hqk,khd->qhd', low(softmax_weights), value_heads, precision=lax.Precision.HIGHEST)
    mixture = lax.map(jax.checkpoint(attend), (queries.reshape(blocks, block_rows, H, HD), position.reshape(blocks, block_rows), segs.reshape(blocks, block_rows)))
    attended = low_back(low(mixture.reshape(TREE, D)))
    middle = inputs + low_back(dense(attended, w_out) + b_out)
    normed_mid = low(norm_rows(middle, second_gain, second_shift))
    hidden = low_back(dense(normed_mid, w_up) + b_up)
    active = low(jax.nn.gelu(hidden, approximate=False))
    return middle + low_back(dense(active, w_down) + b_down)

def reference(tokens, tree_position, segment, parent_table, norm1_gain, norm1_shift, query_weight, query_bias, key_weight, value_weight, value_bias, out_weight, out_bias, norm2_gain, norm2_shift, up_weight, up_bias, down_weight, down_bias, cotangent):
    params = tuple((member.astype(jnp.float32) for member in (norm1_gain, norm1_shift, query_weight, query_bias, key_weight, value_weight, value_bias, out_weight, out_bias, norm2_gain, norm2_shift, up_weight, up_bias, down_weight, down_bias)))
    inputs = tokens.astype(jnp.float32)

    def forward(inputs, params):

        def tree_step(carried, member):
            tree_in, position, segs, parent = member
            return (carried, jax.checkpoint(tree_forward)(params, tree_in, position, segs, parent))
        _, result = lax.scan(tree_step, jnp.zeros((), jnp.float32), (inputs, tree_position, segment, parent_table))
        return result
    result, pullback = jax.vjp(forward, inputs, params)
    grad_inputs, grads = pullback(cotangent.astype(jnp.float32))
    return (result.astype(jnp.bfloat16), grad_inputs.astype(jnp.bfloat16), grads[0], grads[1], grads[2], grads[3], grads[4], grads[5], grads[6], grads[7], grads[8], grads[9], grads[10], grads[11], grads[12], grads[13], grads[14])
```

```python
import math
from functools import partial

import jax
import jax.numpy as jnp
from jax import lax
from jax.experimental import pallas as pl
from jax.experimental.pallas import tpu as pltpu
from jax.sharding import PartitionSpec as P

HD = 128
RUN = 64
TILE = 256
SCALE = 1.0 / math.sqrt(HD)
SCALE2 = SCALE * math.log2(math.e)
NEG = -1e30
EPS = 1e-05
F32 = jnp.float32
BF16 = jnp.bfloat16


def nn(a, b):
    return lax.dot_general(a, b, (((1,), (0,)), ((), ())), preferred_element_type=F32)


def nt(a, b):
    return lax.dot_general(a, b, (((1,), (1,)), ((), ())), preferred_element_type=F32)


def tn(a, b):
    return lax.dot_general(a, b, (((0,), (0,)), ((), ())), preferred_element_type=F32)


def seg_of(pos,starts_ref,t,nseg):
    s=jnp.zeros_like(pos)
    for i in range(1,nseg): s=s+(pos>=starts_ref[t,i]).astype(jnp.int32)
    return s
def path_of(seg,path_ref,t,nseg):
    p=jnp.zeros_like(seg)
    for i in range(nseg): p=jnp.where(seg==i,path_ref[t,i],p)
    return p

def fwd_kernel(nsrc,place,starts,path,code,*refs):
    ins=refs[:nsrc]; outs=refs[nsrc:2*nsrc]; lse_ref=refs[2*nsrc]
    qs,ks,vs,os,kbit,qpath,m_s,l_s,acc_s=refs[2*nsrc+1:]
    t=pl.program_id(0)
    local=ins[0].shape[1]; per=local//RUN; rows=nsrc*local; n=rows//TILE
    nseg=path.shape[1]
    for s in range(nsrc):
        for j in range(per):
            d=pl.multiple_of(place[t,s*per+j]*RUN,RUN)
            blk=ins[s][0,j*RUN:(j+1)*RUN,:]
            qs[pl.ds(d,RUN),:]=blk[:,0:HD]; ks[pl.ds(d,RUN),:]=blk[:,HD:2*HD]; vs[pl.ds(d,RUN),:]=blk[:,2*HD:]
    pos=lax.broadcasted_iota(jnp.int32,(rows,HD),0)
    kbit[...]=jnp.left_shift(1,seg_of(pos,starts,t,nseg))
    qpos=lax.broadcasted_iota(jnp.int32,(n,TILE),0)*TILE+lax.broadcasted_iota(jnp.int32,(n,TILE),1)
    qpath[...]=path_of(seg_of(qpos,starts,t,nseg),path,t,nseg)
    def qloop(qi,_):
        q0=pl.multiple_of(qi*TILE,TILE)
        m_s[...]=jnp.full_like(m_s,NEG); l_s[...]=jnp.zeros_like(l_s); acc_s[...]=jnp.zeros_like(acc_s)
        qt=qs[pl.ds(q0,TILE),:]
        qp=qpath[pl.ds(qi,1),:]
        def kloop(ki,_):
            k0=pl.multiple_of(ki*TILE,TILE)
            c=code[t,qi*n+ki]
            def step(masked):
                sT=nt(ks[pl.ds(k0,TILE),:],qt)
                if masked:
                    kb=kbit[pl.ds(k0,TILE),:]
                    kb=jnp.concatenate([kb]*(TILE//HD),axis=1)
                    diff=(q0-k0)+lax.broadcasted_iota(jnp.int32,(TILE,TILE),1)-lax.broadcasted_iota(jnp.int32,(TILE,TILE),0)
                    vis=((kb&qp)!=0)&(diff>=0)
                    sT=jnp.where(vis,sT,NEG)
                m0=m_s[...]
                m1=jnp.maximum(m0,jnp.max(sT,axis=0,keepdims=True))
                pT=jnp.exp2((sT-m1)*SCALE2)
                al=jnp.exp2((m0-m1)*SCALE2)
                l_s[...]=l_s[...]*al+jnp.sum(pT,axis=0,keepdims=True)
                acc_s[...]=acc_s[...]*al+tn(vs[pl.ds(k0,TILE),:],pT.astype(BF16))
                m_s[...]=m1
            @pl.when(c==2)
            def _(): step(False)
            @pl.when(c==1)
            def _(): step(True)
            return 0
        lax.fori_loop(0,qi+1,kloop,0)
        l=l_s[...]
        os[pl.ds(q0,TILE),:]=jnp.transpose(acc_s[...]/l).astype(BF16)
        lse_ref[0,pl.ds(qi,1),:]=m_s[...]*SCALE2+jnp.log2(l)
        return 0
    lax.fori_loop(0,n,qloop,0)
    for s in range(nsrc):
        for j in range(per):
            d=pl.multiple_of(place[t,s*per+j]*RUN,RUN)
            outs[s][0,j*RUN:(j+1)*RUN,:]=os[pl.ds(d,RUN),:]

def attention_fwd(tables,parts):
    place,starts,path,code=tables
    nsrc=len(parts); T,local,_=parts[0].shape; rows=nsrc*local; n=rows//TILE
    bs=lambda w: pl.BlockSpec((1,local,w),lambda t,*_:(t,0,0))
    return pl.pallas_call(partial(fwd_kernel,nsrc),
        grid_spec=pltpu.PrefetchScalarGridSpec(num_scalar_prefetch=4,grid=(T,),
            in_specs=[bs(3*HD)]*nsrc,
            out_specs=[bs(HD)]*nsrc+[pl.BlockSpec((1,n,TILE),lambda t,*_:(t,0,0))],
            scratch_shapes=[pltpu.VMEM((rows,HD),BF16)]*4+[pltpu.VMEM((rows,HD),jnp.int32),pltpu.VMEM((n,TILE),jnp.int32),
               pltpu.VMEM((1,TILE),F32),pltpu.VMEM((1,TILE),F32),pltpu.VMEM((HD,TILE),F32)]),
        out_shape=[jax.ShapeDtypeStruct((T,local,HD),BF16)]*nsrc+[jax.ShapeDtypeStruct((T,n,TILE),F32)],
        cost_estimate=pl.CostEstimate(flops=T*rows*rows*HD*2,bytes_accessed=T*rows*HD*8,transcendentals=T*rows*rows//2),
        name="tree_attention")(place,starts,path,code,*parts)

def bwd_kernel(nsrc,place,starts,path,code,*refs):
    ins=refs[:nsrc]; oin=refs[nsrc:2*nsrc]; gin=refs[2*nsrc:3*nsrc]; lse_ref=refs[3*nsrc]
    outs=refs[3*nsrc+1:4*nsrc+1]
    qs,ks,vs,gs,os,kbit,qpath,dsum,dq,dk,dv,sorted_out=refs[4*nsrc+1:]
    t=pl.program_id(0)
    local=ins[0].shape[1]; per=local//RUN; rows=nsrc*local; n=rows//TILE
    nseg=path.shape[1]
    for s in range(nsrc):
        for j in range(per):
            d=pl.multiple_of(place[t,s*per+j]*RUN,RUN)
            blk=ins[s][0,j*RUN:(j+1)*RUN,:]
            qs[pl.ds(d,RUN),:]=blk[:,0:HD]; ks[pl.ds(d,RUN),:]=blk[:,HD:2*HD]; vs[pl.ds(d,RUN),:]=blk[:,2*HD:]
            gs[pl.ds(d,RUN),:]=gin[s][0,j*RUN:(j+1)*RUN,:]; os[pl.ds(d,RUN),:]=oin[s][0,j*RUN:(j+1)*RUN,:]
    pos=lax.broadcasted_iota(jnp.int32,(rows,HD),0)
    kbit[...]=jnp.left_shift(1,seg_of(pos,starts,t,nseg))
    qpos=lax.broadcasted_iota(jnp.int32,(n,TILE),0)*TILE+lax.broadcasted_iota(jnp.int32,(n,TILE),1)
    qpath[...]=path_of(seg_of(qpos,starts,t,nseg),path,t,nseg)
    def dloop(qi,_):
        q0=pl.multiple_of(qi*TILE,TILE)
        prod=gs[pl.ds(q0,TILE),:].astype(F32)*os[pl.ds(q0,TILE),:].astype(F32)
        dsum[pl.ds(qi,1),:]=jnp.sum(jnp.transpose(prod),axis=0,keepdims=True)
        return 0
    lax.fori_loop(0,n,dloop,0)
    dq[...]=jnp.zeros_like(dq)
    def kloop(ki,_):
        k0=pl.multiple_of(ki*TILE,TILE)
        kt=ks[pl.ds(k0,TILE),:]; vt=vs[pl.ds(k0,TILE),:]
        dk[...]=jnp.zeros_like(dk); dv[...]=jnp.zeros_like(dv)
        def qloop(qi,_):
            q0=pl.multiple_of(qi*TILE,TILE)
            c=code[t,qi*n+ki]
            def step(masked):
                qt=qs[pl.ds(q0,TILE),:]; gt=gs[pl.ds(q0,TILE),:]
                sT=nt(kt,qt)
                dpT=nt(vt,gt)
                pT=jnp.exp2(sT*SCALE2-lse_ref[0,pl.ds(qi,1),:])
                if masked:
                    kb=kbit[pl.ds(k0,TILE),:]
                    kb=jnp.concatenate([kb]*(TILE//HD),axis=1)
                    qp=qpath[pl.ds(qi,1),:]
                    diff=(q0-k0)+lax.broadcasted_iota(jnp.int32,(TILE,TILE),1)-lax.broadcasted_iota(jnp.int32,(TILE,TILE),0)
                    vis=((kb&qp)!=0)&(diff>=0)
                    pT=jnp.where(vis,pT,0.0)
                dsT=(pT*(dpT-dsum[pl.ds(qi,1),:])).astype(BF16)
                dv[...]+=nn(pT.astype(BF16),gt)
                dk[...]+=nn(dsT,qt)
                dq[pl.ds(q0,TILE),:]+=tn(dsT,kt)
            @pl.when(c==2)
            def _(): step(False)
            @pl.when(c==1)
            def _(): step(True)
            return 0
        lax.fori_loop(ki,n,qloop,0)
        sorted_out[pl.ds(k0,TILE),HD:2*HD]=(dk[...]*SCALE).astype(BF16)
        sorted_out[pl.ds(k0,TILE),2*HD:]=dv[...].astype(BF16)
        return 0
    lax.fori_loop(0,n,kloop,0)
    sorted_out[:,0:HD]=(dq[...]*SCALE).astype(BF16)
    for s in range(nsrc):
        for j in range(per):
            d=pl.multiple_of(place[t,s*per+j]*RUN,RUN)
            outs[s][0,j*RUN:(j+1)*RUN,:]=sorted_out[pl.ds(d,RUN),:]

def attention_bwd(tables,parts,oparts,gparts,lse):
    place,starts,path,code=tables
    nsrc=len(parts); T,local,_=parts[0].shape; rows=nsrc*local; n=rows//TILE
    bs=lambda w: pl.BlockSpec((1,local,w),lambda t,*_:(t,0,0))
    return pl.pallas_call(partial(bwd_kernel,nsrc),
        grid_spec=pltpu.PrefetchScalarGridSpec(num_scalar_prefetch=4,grid=(T,),
            in_specs=[bs(3*HD)]*nsrc+[bs(HD)]*(2*nsrc)+[pl.BlockSpec((1,n,TILE),lambda t,*_:(t,0,0))],
            out_specs=[bs(3*HD)]*nsrc,
            scratch_shapes=[pltpu.VMEM((rows,HD),BF16)]*5+[pltpu.VMEM((rows,HD),jnp.int32),pltpu.VMEM((n,TILE),jnp.int32),
               pltpu.VMEM((n,TILE),F32),pltpu.VMEM((rows,HD),F32),pltpu.VMEM((TILE,HD),F32),pltpu.VMEM((TILE,HD),F32),
               pltpu.VMEM((rows,3*HD),BF16)]),
        out_shape=[jax.ShapeDtypeStruct((T,local,3*HD),BF16)]*nsrc,
        cost_estimate=pl.CostEstimate(flops=T*rows*rows*HD*5,bytes_accessed=T*rows*HD*20,transcendentals=T*rows*rows//2),
        name="tree_attention_back")(place,starts,path,code,*parts,*oparts,*gparts,lse)


def tree_tables(place, starts, parent, rows):
    labels = jnp.arange(parent.shape[1], dtype=jnp.int32)
    second = jnp.sum(jnp.where(parent[:, :, None] == labels, parent[:, None, :], 0), axis=2)
    path = (1 << labels)[None] | (1 << parent) | (1 << second)
    tiles = rows // TILE
    first_row = jnp.arange(tiles, dtype=jnp.int32)[None, :, None] * TILE
    low = jnp.sum((first_row >= starts[:, None, :]).astype(jnp.int32), axis=2) - 1
    high = jnp.sum((first_row + TILE - 1 >= starts[:, None, :]).astype(jnp.int32), axis=2) - 1
    inside = (labels >= low[:, :, None]) & (labels <= high[:, :, None])
    see = ((path[:, :, None] >> labels) & 1) == 1
    pair = inside[:, :, None, :, None] & inside[:, None, :, None, :]
    some = jnp.any(pair & see[:, None, None], axis=(3, 4))
    every = jnp.all((~pair) | see[:, None, None], axis=(3, 4))
    query = jnp.arange(tiles)[:, None]
    key = jnp.arange(tiles)[None, :]
    code = jnp.where((key > query) | ~some, 0, jnp.where(every & (key < query), 2, 1))
    return (
        place.astype(jnp.int32),
        starts.astype(jnp.int32),
        path.astype(jnp.int32),
        code.astype(jnp.int32).reshape(-1, tiles * tiles),
    )


def hypercube(n):
    bits = n.bit_length() - 1
    order = [sum(((r >> b) & 1) << (bits - 1 - b) for b in range(bits)) for r in range(n)]
    return bits, order


def first_norm_kernel(pieces, quarter, chunk, x_ref, dy_ref, gain_ref, shift_ref, n_ref, x0_ref, dyr_ref):
    width = x_ref.shape[2]
    part = width // pieces
    x = x_ref[0].astype(F32)
    mean = jnp.mean(x, axis=1, keepdims=True)
    spread = jnp.mean((x - mean) * (x - mean), axis=1, keepdims=True)
    scale = lax.rsqrt(spread + EPS)
    for k in range(pieces):
        here = slice(k * part, (k + 1) * part)
        there = pl.ds(pl.multiple_of(chunk[k] * part, part), part)
        xk = x_ref[0, :, there]
        n_ref[0, :, here] = (
            (xk.astype(F32) - mean) * scale * gain_ref[:, here] + shift_ref[:, here]
        ).astype(BF16)
        dyr_ref[0, :, here] = dy_ref[0, :, there]

        @pl.when(pl.program_id(1) == 0)
        def _():
            x0_ref[0, :, here] = xk


def first_norm(quarter, chunk, tokens, cotangent, gain, shift):
    trees, rows, width = tokens.shape
    parts = quarter.shape[0]
    block = (1, rows // parts, width)
    come = pl.BlockSpec(block, lambda i, r, q, c: (i, q[r], 0))
    go = pl.BlockSpec(block, lambda i, r, q, c: (i, r, 0))
    row = pl.BlockSpec((1, width), lambda i, r, q, c: (0, 0))
    return pl.pallas_call(
        partial(first_norm_kernel, chunk.shape[0]),
        grid_spec=pltpu.PrefetchScalarGridSpec(
            num_scalar_prefetch=2,
            grid=(trees, parts),
            in_specs=[come, come, row, row],
            out_specs=[go, pl.BlockSpec(block, lambda i, r, q, c: (i, 0, 0)), go],
        ),
        out_shape=[
            jax.ShapeDtypeStruct((trees, rows, width), BF16),
            jax.ShapeDtypeStruct((trees, rows // parts, width), BF16),
            jax.ShapeDtypeStruct((trees, rows, width), BF16),
        ],
        cost_estimate=pl.CostEstimate(
            flops=10 * tokens.size, bytes_accessed=8 * tokens.size, transcendentals=0
        ),
        name="first_norm",
    )(quarter, chunk, tokens, cotangent, gain, shift)


def replace_kernel(pieces, quarter, chunk, x_ref, o_ref):
    part = x_ref.shape[1] // pieces
    for k in range(pieces):
        there = pl.ds(pl.multiple_of(chunk[k] * part, part), part)
        o_ref[:, there] = x_ref[:, k * part : (k + 1) * part]


def replace(quarter, chunk, value):
    rows, width = value.shape
    parts = quarter.shape[0]
    block = (rows // parts, width)
    return pl.pallas_call(
        partial(replace_kernel, chunk.shape[0]),
        grid_spec=pltpu.PrefetchScalarGridSpec(
            num_scalar_prefetch=2,
            grid=(parts,),
            in_specs=[pl.BlockSpec(block, lambda r, q, c: (r, 0))],
            out_specs=pl.BlockSpec(block, lambda r, q, c: (q[r], 0)),
        ),
        out_shape=jax.ShapeDtypeStruct((rows, width), value.dtype),
        cost_estimate=pl.CostEstimate(flops=0, bytes_accessed=4 * value.size, transcendentals=0),
        name="replace",
    )(quarter, chunk, value)


def per_device(
    sizes,
    tokens,
    tree_position,
    segment,
    parent_table,
    norm1_gain,
    norm1_shift,
    query_weight,
    query_bias,
    key_weight,
    value_weight,
    value_bias,
    out_weight,
    out_bias,
    norm2_gain,
    norm2_shift,
    up_weight,
    up_bias,
    down_weight,
    down_bias,
    cotangent,
):
    n_f, n_c, n_t = sizes["fsdp"], sizes["ctx"], sizes["tp"]
    f, c, t = (lax.axis_index(name) for name in ("fsdp", "ctx", "tp"))
    trees, rows, width = tokens.shape
    part = width // n_f
    local_width = query_weight.shape[1]
    heads = local_width // HD
    mine = heads // n_c
    bits, order = hypercube(n_t)
    quarter_rows = rows // n_t

    def shift_f(v, k):
        return lax.ppermute(v, "fsdp", [(i, (i + k) % n_f) for i in range(n_f)])

    def shift_c(v, k):
        return lax.ppermute(v, "ctx", [(i, (i + k) % n_c) for i in range(n_c)])

    def flip_t(v, b):
        return lax.ppermute(v, "tp", [(i, i ^ (1 << b)) for i in range(n_t)])

    def pieces_of(v):
        return [v] + [shift_f(v, -k) for k in range(1, n_f)]

    def sum_rows(v):
        for b in range(bits):
            half = v.shape[0] // 2
            come = flip_t(v[half:].astype(BF16), b)
            v = v[:half].astype(F32) + come.astype(F32)
        return v

    def all_rows(v):
        for b in reversed(range(bits)):
            v = jnp.concatenate([v, flip_t(v, b)], axis=0)
        return v

    quarter = jnp.stack([t ^ r for r in order]).astype(jnp.int32)
    chunk = jnp.stack([(f + k) % n_f for k in range(n_f)]).astype(jnp.int32)

    def roll_in(v):
        return jnp.concatenate(
            [lax.dynamic_slice_in_dim(v, chunk[k] * part, part, axis=-1) for k in range(n_f)], axis=-1
        )

    vectors = roll_in(
        jnp.stack([norm1_gain, norm1_shift, norm2_gain, norm2_shift, out_bias, down_bias])
    )
    gain1, shift1, gain2, shift2, bias_out, bias_down = (vectors[i : i + 1] for i in range(6))

    def by_head(q, k, v):
        stacked = jnp.stack([a.reshape(a.shape[0], heads, HD) for a in (q, k, v)], axis=2)
        doubled = jnp.concatenate([stacked, stacked], axis=1)
        turned = lax.dynamic_slice_in_dim(doubled, c * mine, heads, axis=1)
        return turned.reshape(q.shape[0], heads * 3 * HD)

    w_qkv = pieces_of(by_head(query_weight, key_weight, value_weight))
    w_out = jnp.concatenate([out_weight, out_weight], axis=0)
    w_out = pieces_of(lax.dynamic_slice_in_dim(w_out, c * mine * HD, local_width, axis=0))
    w_up = pieces_of(up_weight)
    w_down = pieces_of(down_weight)
    bias_qkv = by_head(query_bias[None], jnp.zeros_like(query_bias)[None], value_bias[None])

    n_seg = parent_table.shape[1]

    def relative(v):
        blocks = v.reshape(trees, n_t, quarter_rows)
        return jnp.concatenate(
            [lax.dynamic_slice_in_dim(blocks, quarter[r], 1, axis=1) for r in range(n_t)], axis=1
        ).reshape(trees, rows)

    places = relative(tree_position)[:, ::RUN] // RUN
    ahead = jnp.sum(
        (segment[:, None, :] < jnp.arange(n_seg, dtype=jnp.int32)[None, :, None]).astype(jnp.int32), axis=2
    )
    info = jnp.concatenate([places, ahead], axis=1)
    infos = [info] + [shift_c(info, k) for k in range(1, n_c)]
    runs = places.shape[1]
    place = jnp.concatenate([v[:, :runs] for v in infos], axis=1)
    starts = sum(v[:, runs:] for v in infos)
    tables = tree_tables(place, starts, parent_table, n_c * rows)

    normed, inputs0, dy = first_norm(quarter, chunk, tokens, cotangent, gain1, shift1)

    def cols(v, k):
        return v[:, k * part : (k + 1) * part]

    def times(v, pieces):
        return sum(nn(cols(v, k), pieces[k]) for k in range(n_f))

    def times_back(v, pieces):
        return sum(nt(cols(v, k), pieces[k]) for k in range(n_f))

    def wide(v, pieces):
        return jnp.concatenate([nn(v, p) for p in pieces], axis=1)

    def wide_back(v, pieces):
        return jnp.concatenate([nt(v, p) for p in pieces], axis=1)

    def to_heads(v, width_each):
        span = mine * width_each
        return [v[:, :span]] + [shift_c(v[:, k * span : (k + 1) * span], k) for k in range(1, n_c)]

    def from_heads(parts):
        return [parts[0]] + [shift_c(parts[k], -k) for k in range(1, n_c)]

    def absolute(parts):
        doubled = jnp.stack(parts + parts)
        turned = lax.dynamic_slice_in_dim(doubled, (n_c - c) % n_c, n_c, axis=0)
        return jnp.concatenate([turned[k] for k in range(n_c)], axis=1)

    kept = []
    for i in range(trees):
        table = tuple(v[i : i + 1] for v in tables)
        qkv = (times(normed[i], w_qkv) + bias_qkv).astype(BF16)
        parts = to_heads(qkv, 3 * HD)
        parts = [v[None] for v in parts]
        *attended_parts, lse = attention_fwd(table, parts)
        attended = from_heads([v[0] for v in attended_parts])
        attended_here = jnp.concatenate(attended, axis=1)
        x0 = inputs0[i].astype(F32)
        middle = x0 + sum_rows(wide(attended_here, w_out)) + bias_out
        mean = jnp.mean(middle, axis=1, keepdims=True)
        spread = jnp.mean((middle - mean) * (middle - mean), axis=1, keepdims=True)
        rstd = lax.rsqrt(spread + EPS)
        unit = (middle - mean) * rstd
        normed_mid = all_rows((unit * gain2 + shift2).astype(BF16))
        kept.append((table, parts, attended_parts, lse, attended, x0, middle, unit, rstd, normed_mid))

    results = []
    back = []
    for i in range(trees):
        table, parts, attended_parts, lse, attended, x0, middle, unit, rstd, normed_mid = kept[i]
        hidden = times(normed_mid, w_up) + up_bias[None]
        cdf = 0.5 * (1.0 + lax.erf(hidden * math.sqrt(0.5)))
        slope = cdf + hidden * (jnp.exp(-0.5 * hidden * hidden) * (1.0 / math.sqrt(2.0 * math.pi)))
        active = (hidden * cdf).astype(BF16)
        grad_hidden = (times_back(dy[i], w_down) * slope).astype(BF16)
        grad_mid = sum_rows(wide_back(grad_hidden, w_up))
        g = grad_mid * gain2
        moved = rstd * (
            g - jnp.mean(g, axis=1, keepdims=True) - unit * jnp.mean(g * unit, axis=1, keepdims=True)
        )
        grad_middle = dy[i, :quarter_rows].astype(F32) + moved
        branch0 = grad_middle.astype(BF16)
        branch = all_rows(branch0)
        result = middle + sum_rows(wide(active, w_down)) + bias_down
        results.append(all_rows(result.astype(BF16)))
        back.append(
            dict(
                active=active,
                grad_hidden=grad_hidden,
                normed_mid=normed_mid,
                branch=branch,
                grad_middle=grad_middle,
                gain2=jnp.sum(grad_mid * unit, axis=0),
                shift2=jnp.sum(grad_mid, axis=0),
                out_bias=jnp.sum(branch0.astype(F32), axis=0),
                down_bias=jnp.sum(dy[i, :quarter_rows].astype(F32), axis=0),
                up_bias=jnp.sum(grad_hidden.astype(F32), axis=0),
            )
        )

    def whole(name):
        return jnp.concatenate([b[name] for b in back], axis=0)

    def scatter(parts, axis):
        total = parts[0].astype(F32)
        for k in range(1, n_f):
            total = total + shift_f(parts[k].astype(BF16), k).astype(F32)
        return lax.psum_scatter(
            total.astype(BF16), "ctx", scatter_dimension=axis, tiled=True
        ).astype(F32)

    dys = dy.reshape(trees * rows, width)
    active, grad_hidden, normed_mid = whole("active"), whole("grad_hidden"), whole("normed_mid")
    g_down = scatter([tn(active, cols(dys, k)) for k in range(n_f)], 1)
    g_up = scatter([tn(cols(normed_mid, k), grad_hidden) for k in range(n_f)], 0)

    heads_back = []
    for i in range(trees):
        table, parts, attended_parts, lse, attended, x0 = kept[i][:6]
        grad_attended = times_back(back[i]["branch"], w_out).astype(BF16)
        grad_parts = [v[None] for v in to_heads(grad_attended, HD)]
        back_parts = attention_bwd(table, parts, attended_parts, grad_parts, lse)
        heads_back.append(from_heads([v[0] for v in back_parts]))

    branch = whole("branch")
    attended_abs = jnp.concatenate([absolute(k[4]) for k in kept], axis=0)
    g_out = scatter([tn(attended_abs, cols(branch, k)) for k in range(n_f)], 1)

    grads = []
    for i in range(trees):
        x0, grad_middle = kept[i][5], back[i]["grad_middle"]
        g = sum_rows(wide_back(jnp.concatenate(heads_back[i], axis=1), w_qkv))
        mean = jnp.mean(x0, axis=1, keepdims=True)
        spread = jnp.mean((x0 - mean) * (x0 - mean), axis=1, keepdims=True)
        rstd = lax.rsqrt(spread + EPS)
        unit = (x0 - mean) * rstd
        back[i]["gain1"] = jnp.sum(g * unit, axis=0)
        back[i]["shift1"] = jnp.sum(g, axis=0)
        g = g * gain1
        moved = rstd * (
            g - jnp.mean(g, axis=1, keepdims=True) - unit * jnp.mean(g * unit, axis=1, keepdims=True)
        )
        grads.append(all_rows((grad_middle + moved).astype(BF16)))

    dqkv = jnp.concatenate([absolute(v) for v in heads_back], axis=0)
    normed_all = normed.reshape(trees * rows, width)
    g_qkv = scatter([tn(cols(normed_all, k), dqkv) for k in range(n_f)], 0)
    bias_sums = jnp.sum(dqkv.astype(F32), axis=0)

    def split_heads(v):
        apart = v.reshape(v.shape[0], heads, 3, HD)
        return [apart[:, :, k].reshape(v.shape[0], heads * HD) for k in range(3)]

    g_query, g_key, g_value = split_heads(g_qkv)
    query_sum, _, value_sum = split_heads(bias_sums[None])
    names = ("gain1", "shift1", "out_bias", "gain2", "shift2", "down_bias")
    rolled = jnp.stack([sum(b[name] for b in back) for name in names])
    turned = jnp.concatenate(
        [
            lax.dynamic_slice_in_dim(rolled, ((n_f + k - f) % n_f) * part, part, axis=1)
            for k in range(n_f)
        ],
        axis=1,
    )
    turned = lax.psum(turned, ("fsdp", "ctx", "tp"))
    span = part // n_c
    own = lax.dynamic_slice_in_dim(turned, f * part + c * span, span, axis=1)
    unit_sums = jnp.concatenate(
        [query_sum[0], value_sum[0], sum(b["up_bias"] for b in back)], axis=0
    )
    unit_sums = lax.psum(unit_sums, ("fsdp", "ctx"))
    return (
        jnp.stack([replace(quarter, chunk, v) for v in results]),
        jnp.stack([replace(quarter, chunk, v) for v in grads]),
        own[0],
        own[1],
        g_query,
        unit_sums[:local_width],
        g_key,
        g_value,
        unit_sums[local_width : 2 * local_width],
        g_out,
        own[2],
        own[3],
        own[4],
        g_up,
        unit_sums[2 * local_width :],
        g_down,
        own[5],
    )


def solution(mesh):
    in_specs = (
        P("fsdp", "ctx", None),
        P("fsdp", "ctx"),
        P("fsdp", "ctx"),
        P("fsdp", None),
        P(),
        P(),
        P("fsdp", "tp"),
        P("tp"),
        P("fsdp", "tp"),
        P("fsdp", "tp"),
        P("tp"),
        P("tp", "fsdp"),
        P(),
        P(),
        P(),
        P("fsdp", "tp"),
        P("tp"),
        P("tp", "fsdp"),
        P(),
        P("fsdp", "ctx", None),
    )
    out_specs = (
        P("fsdp", "ctx", None),
        P("fsdp", "ctx", None),
        P(("fsdp", "ctx")),
        P(("fsdp", "ctx")),
        P(("fsdp", "ctx"), "tp"),
        P("tp"),
        P(("fsdp", "ctx"), "tp"),
        P(("fsdp", "ctx"), "tp"),
        P("tp"),
        P("tp", ("fsdp", "ctx")),
        P(("fsdp", "ctx")),
        P(("fsdp", "ctx")),
        P(("fsdp", "ctx")),
        P(("fsdp", "ctx"), "tp"),
        P("tp"),
        P("tp", ("fsdp", "ctx")),
        P(("fsdp", "ctx")),
    )
    return jax.shard_map(
        partial(per_device, dict(mesh.shape)), mesh=mesh, in_specs=in_specs, out_specs=out_specs, check_vma=False
    )
```

```python
import math
from functools import partial

import jax
import jax.numpy as jnp
from jax import lax
from jax.experimental import pallas as pl
from jax.experimental.pallas import tpu as pltpu
from jax.sharding import PartitionSpec as P

HD = 128
RUN = 64
TILE = 256
SCALE = 1.0 / math.sqrt(HD)
SCALE2 = SCALE * math.log2(math.e)
NEG = -1e30
EPS = 1e-05
F32 = jnp.float32
BF16 = jnp.bfloat16


def nn(a, b):
    return lax.dot_general(a, b, (((1,), (0,)), ((), ())), preferred_element_type=F32)


def nt(a, b):
    return lax.dot_general(a, b, (((1,), (1,)), ((), ())), preferred_element_type=F32)


def tn(a, b):
    return lax.dot_general(a, b, (((0,), (0,)), ((), ())), preferred_element_type=F32)


def seg_of(pos,starts_ref,t,nseg):
    s=jnp.zeros_like(pos)
    for i in range(1,nseg): s=s+(pos>=starts_ref[t,i]).astype(jnp.int32)
    return s
def path_of(seg,path_ref,t,nseg):
    p=jnp.zeros_like(seg)
    for i in range(nseg): p=jnp.where(seg==i,path_ref[t,i],p)
    return p

def fwd_kernel(nsrc,place,starts,path,code,*refs):
    qkv_ref=refs[0]; outs=refs[1:nsrc+1]; lse_ref=refs[nsrc+1]
    qs,ks,vs,os,kbit,qpath,m_s,l_s,acc_s=refs[nsrc+2:]
    t=pl.program_id(0)
    rows=qkv_ref.shape[1]; local=rows//nsrc; per=local//RUN; n=rows//TILE
    nseg=path.shape[1]
    for s in range(nsrc):
        for j in range(per):
            d=pl.multiple_of(place[t,s*per+j]*RUN,RUN)
            blk=qkv_ref[0,s*local+j*RUN:s*local+(j+1)*RUN,:]
            qs[pl.ds(d,RUN),:]=blk[:,0:HD]; ks[pl.ds(d,RUN),:]=blk[:,HD:2*HD]; vs[pl.ds(d,RUN),:]=blk[:,2*HD:]
    pos=lax.broadcasted_iota(jnp.int32,(rows,HD),0)
    kbit[...]=jnp.left_shift(1,seg_of(pos,starts,t,nseg))
    qpos=lax.broadcasted_iota(jnp.int32,(n,TILE),0)*TILE+lax.broadcasted_iota(jnp.int32,(n,TILE),1)
    qpath[...]=path_of(seg_of(qpos,starts,t,nseg),path,t,nseg)
    def qloop(qi,_):
        q0=pl.multiple_of(qi*TILE,TILE)
        m_s[...]=jnp.full_like(m_s,NEG); l_s[...]=jnp.zeros_like(l_s); acc_s[...]=jnp.zeros_like(acc_s)
        qt=qs[pl.ds(q0,TILE),:]
        qp=qpath[pl.ds(qi,1),:]
        def kloop(ki,_):
            k0=pl.multiple_of(ki*TILE,TILE)
            c=code[t,qi*n+ki]
            def step(masked):
                sT=nt(ks[pl.ds(k0,TILE),:],qt)
                if masked:
                    kb=kbit[pl.ds(k0,TILE),:]
                    kb=jnp.concatenate([kb]*(TILE//HD),axis=1)
                    diff=(q0-k0)+lax.broadcasted_iota(jnp.int32,(TILE,TILE),1)-lax.broadcasted_iota(jnp.int32,(TILE,TILE),0)
                    vis=((kb&qp)!=0)&(diff>=0)
                    sT=jnp.where(vis,sT,NEG)
                m0=m_s[...]
                m1=jnp.maximum(m0,jnp.max(sT,axis=0,keepdims=True))
                pT=jnp.exp2((sT-m1)*SCALE2)
                al=jnp.exp2((m0-m1)*SCALE2)
                l_s[...]=l_s[...]*al+jnp.sum(pT,axis=0,keepdims=True)
                acc_s[...]=acc_s[...]*al+tn(vs[pl.ds(k0,TILE),:],pT.astype(BF16))
                m_s[...]=m1
            @pl.when(c==2)
            def _(): step(False)
            @pl.when(c==1)
            def _(): step(True)
            return 0
        lax.fori_loop(0,qi+1,kloop,0)
        l=l_s[...]
        os[pl.ds(q0,TILE),:]=jnp.transpose(acc_s[...]/l).astype(BF16)
        lse_ref[0,pl.ds(qi,1),:]=m_s[...]*SCALE2+jnp.log2(l)
        return 0
    lax.fori_loop(0,n,qloop,0)
    for s in range(nsrc):
        for j in range(per):
            d=pl.multiple_of(place[t,s*per+j]*RUN,RUN)
            outs[s][0,j*RUN:(j+1)*RUN,:]=os[pl.ds(d,RUN),:]

def attention_fwd(tables,nsrc,qkv):
    place,starts,path,code=tables
    T,rows,_=qkv.shape; local=rows//nsrc; n=rows//TILE
    bs=lambda w: pl.BlockSpec((1,local,w),lambda t,*_:(t,0,0))
    return pl.pallas_call(partial(fwd_kernel,nsrc),
        grid_spec=pltpu.PrefetchScalarGridSpec(num_scalar_prefetch=4,grid=(T,),
            in_specs=[pl.BlockSpec((1,rows,3*HD),lambda t,*_:(t,0,0))],
            out_specs=[bs(HD)]*nsrc+[pl.BlockSpec((1,n,TILE),lambda t,*_:(t,0,0))],
            scratch_shapes=[pltpu.VMEM((rows,HD),BF16)]*4+[pltpu.VMEM((rows,HD),jnp.int32),pltpu.VMEM((n,TILE),jnp.int32),
               pltpu.VMEM((1,TILE),F32),pltpu.VMEM((1,TILE),F32),pltpu.VMEM((HD,TILE),F32)]),
        out_shape=[jax.ShapeDtypeStruct((T,local,HD),BF16)]*nsrc+[jax.ShapeDtypeStruct((T,n,TILE),F32)],
        cost_estimate=pl.CostEstimate(flops=T*rows*rows*HD*20,bytes_accessed=T*rows*HD*8,transcendentals=T*rows*rows//2),
        name="tree_attention")(place,starts,path,code,qkv)

def bwd_kernel(nsrc,place,starts,path,code,*refs):
    qkv_ref=refs[0]; oin=refs[1:nsrc+1]; gin=refs[nsrc+1:2*nsrc+1]; lse_ref=refs[2*nsrc+1]
    outs=refs[2*nsrc+2:3*nsrc+1]; whole_ref=refs[3*nsrc+1]
    qs,ks,vs,gs,os,kbit,qpath,dsum,dq,dk,dv,sorted_out=refs[3*nsrc+2:]
    t=pl.program_id(0)
    rows=qkv_ref.shape[1]; local=rows//nsrc; per=local//RUN; n=rows//TILE
    nseg=path.shape[1]
    for s in range(nsrc):
        for j in range(per):
            d=pl.multiple_of(place[t,s*per+j]*RUN,RUN)
            blk=qkv_ref[0,s*local+j*RUN:s*local+(j+1)*RUN,:]
            qs[pl.ds(d,RUN),:]=blk[:,0:HD]; ks[pl.ds(d,RUN),:]=blk[:,HD:2*HD]; vs[pl.ds(d,RUN),:]=blk[:,2*HD:]
            gs[pl.ds(d,RUN),:]=gin[s][0,j*RUN:(j+1)*RUN,:]; os[pl.ds(d,RUN),:]=oin[s][0,j*RUN:(j+1)*RUN,:]
    pos=lax.broadcasted_iota(jnp.int32,(rows,HD),0)
    kbit[...]=jnp.left_shift(1,seg_of(pos,starts,t,nseg))
    qpos=lax.broadcasted_iota(jnp.int32,(n,TILE),0)*TILE+lax.broadcasted_iota(jnp.int32,(n,TILE),1)
    qpath[...]=path_of(seg_of(qpos,starts,t,nseg),path,t,nseg)
    def dloop(qi,_):
        q0=pl.multiple_of(qi*TILE,TILE)
        prod=gs[pl.ds(q0,TILE),:].astype(F32)*os[pl.ds(q0,TILE),:].astype(F32)
        dsum[pl.ds(qi,1),:]=jnp.sum(jnp.transpose(prod),axis=0,keepdims=True)
        return 0
    lax.fori_loop(0,n,dloop,0)
    dq[...]=jnp.zeros_like(dq)
    def kloop(ki,_):
        k0=pl.multiple_of(ki*TILE,TILE)
        kt=ks[pl.ds(k0,TILE),:]; vt=vs[pl.ds(k0,TILE),:]
        dk[...]=jnp.zeros_like(dk); dv[...]=jnp.zeros_like(dv)
        def qloop(qi,_):
            q0=pl.multiple_of(qi*TILE,TILE)
            c=code[t,qi*n+ki]
            def step(masked):
                qt=qs[pl.ds(q0,TILE),:]; gt=gs[pl.ds(q0,TILE),:]
                sT=nt(kt,qt)
                dpT=nt(vt,gt)
                pT=jnp.exp2(sT*SCALE2-lse_ref[0,pl.ds(qi,1),:])
                if masked:
                    kb=kbit[pl.ds(k0,TILE),:]
                    kb=jnp.concatenate([kb]*(TILE//HD),axis=1)
                    qp=qpath[pl.ds(qi,1),:]
                    diff=(q0-k0)+lax.broadcasted_iota(jnp.int32,(TILE,TILE),1)-lax.broadcasted_iota(jnp.int32,(TILE,TILE),0)
                    vis=((kb&qp)!=0)&(diff>=0)
                    pT=jnp.where(vis,pT,0.0)
                dsT=(pT*(dpT-dsum[pl.ds(qi,1),:])).astype(BF16)
                dv[...]+=nn(pT.astype(BF16),gt)
                dk[...]+=nn(dsT,qt)
                dq[pl.ds(q0,TILE),:]+=tn(dsT,kt)
            @pl.when(c==2)
            def _(): step(False)
            @pl.when(c==1)
            def _(): step(True)
            return 0
        lax.fori_loop(ki,n,qloop,0)
        sorted_out[pl.ds(k0,TILE),HD:2*HD]=(dk[...]*SCALE).astype(BF16)
        sorted_out[pl.ds(k0,TILE),2*HD:]=dv[...].astype(BF16)
        return 0
    lax.fori_loop(0,n,kloop,0)
    sorted_out[:,0:HD]=(dq[...]*SCALE).astype(BF16)
    for s in range(nsrc):
        for j in range(per):
            d=pl.multiple_of(place[t,s*per+j]*RUN,RUN)
            blk=sorted_out[pl.ds(d,RUN),:]
            whole_ref[0,s*local+j*RUN:s*local+(j+1)*RUN,:]=blk
            if s: outs[s-1][0,j*RUN:(j+1)*RUN,:]=blk

def attention_bwd(tables,qkv,oparts,gparts,lse):
    place,starts,path,code=tables
    nsrc=len(oparts); T,rows,_=qkv.shape; local=rows//nsrc; n=rows//TILE
    bs=lambda w: pl.BlockSpec((1,local,w),lambda t,*_:(t,0,0))
    return pl.pallas_call(partial(bwd_kernel,nsrc),
        grid_spec=pltpu.PrefetchScalarGridSpec(num_scalar_prefetch=4,grid=(T,),
            in_specs=[pl.BlockSpec((1,rows,3*HD),lambda t,*_:(t,0,0))]+[bs(HD)]*(2*nsrc)+[pl.BlockSpec((1,n,TILE),lambda t,*_:(t,0,0))],
            out_specs=[bs(3*HD)]*(nsrc-1)+[pl.BlockSpec((1,rows,3*HD),lambda t,*_:(t,0,0))],
            scratch_shapes=[pltpu.VMEM((rows,HD),BF16)]*5+[pltpu.VMEM((rows,HD),jnp.int32),pltpu.VMEM((n,TILE),jnp.int32),
               pltpu.VMEM((n,TILE),F32),pltpu.VMEM((rows,HD),F32),pltpu.VMEM((TILE,HD),F32),pltpu.VMEM((TILE,HD),F32),
               pltpu.VMEM((rows,3*HD),BF16)]),
        out_shape=[jax.ShapeDtypeStruct((T,local,3*HD),BF16)]*(nsrc-1)+[jax.ShapeDtypeStruct((T,rows,3*HD),BF16)],
        cost_estimate=pl.CostEstimate(flops=T*rows*rows*HD*25,bytes_accessed=T*rows*HD*20,transcendentals=T*rows*rows//2),
        name="tree_attention_back")(place,starts,path,code,qkv,*oparts,*gparts,lse)


def tree_tables(place, starts, parent, rows):
    labels = jnp.arange(parent.shape[1], dtype=jnp.int32)
    second = jnp.sum(jnp.where(parent[:, :, None] == labels, parent[:, None, :], 0), axis=2)
    path = (1 << labels)[None] | (1 << parent) | (1 << second)
    tiles = rows // TILE
    first_row = jnp.arange(tiles, dtype=jnp.int32)[None, :, None] * TILE
    low = jnp.sum((first_row >= starts[:, None, :]).astype(jnp.int32), axis=2) - 1
    high = jnp.sum((first_row + TILE - 1 >= starts[:, None, :]).astype(jnp.int32), axis=2) - 1
    inside = (labels >= low[:, :, None]) & (labels <= high[:, :, None])
    see = ((path[:, :, None] >> labels) & 1) == 1
    pair = inside[:, :, None, :, None] & inside[:, None, :, None, :]
    some = jnp.any(pair & see[:, None, None], axis=(3, 4))
    every = jnp.all((~pair) | see[:, None, None], axis=(3, 4))
    query = jnp.arange(tiles)[:, None]
    key = jnp.arange(tiles)[None, :]
    code = jnp.where((key > query) | ~some, 0, jnp.where(every & (key < query), 2, 1))
    return (
        place.astype(jnp.int32),
        starts.astype(jnp.int32),
        path.astype(jnp.int32),
        code.astype(jnp.int32).reshape(-1, tiles * tiles),
    )


def hypercube(n):
    bits = n.bit_length() - 1
    order = [sum(((r >> b) & 1) << (bits - 1 - b) for b in range(bits)) for r in range(n)]
    return bits, order


def first_norm_kernel(pieces, quarter, chunk, x_ref, dy_ref, gain_ref, shift_ref, n_ref, x0_ref, dyr_ref):
    width = x_ref.shape[2]
    part = width // pieces
    x = x_ref[0].astype(F32)
    mean = jnp.mean(x, axis=1, keepdims=True)
    spread = jnp.mean((x - mean) * (x - mean), axis=1, keepdims=True)
    scale = lax.rsqrt(spread + EPS)
    for k in range(pieces):
        here = slice(k * part, (k + 1) * part)
        there = pl.ds(pl.multiple_of(chunk[k] * part, part), part)
        xk = x_ref[0, :, there]
        n_ref[0, :, here] = (
            (xk.astype(F32) - mean) * scale * gain_ref[:, here] + shift_ref[:, here]
        ).astype(BF16)
        dyr_ref[0, :, here] = dy_ref[0, :, there]

        @pl.when(pl.program_id(1) == 0)
        def _():
            x0_ref[0, :, here] = xk


def first_norm(quarter, chunk, tokens, cotangent, gain, shift, block_rows):
    trees, _, width = tokens.shape
    parts = quarter.shape[0]
    rows = parts * block_rows
    block = (1, block_rows, width)
    come = pl.BlockSpec(block, lambda i, r, q, c: (i, q[r], 0))
    go = pl.BlockSpec(block, lambda i, r, q, c: (i, r, 0))
    row = pl.BlockSpec((1, width), lambda i, r, q, c: (0, 0))
    return pl.pallas_call(
        partial(first_norm_kernel, chunk.shape[0]),
        grid_spec=pltpu.PrefetchScalarGridSpec(
            num_scalar_prefetch=2,
            grid=(trees, parts),
            in_specs=[come, come, row, row],
            out_specs=[go, pl.BlockSpec(block, lambda i, r, q, c: (i, 0, 0)), go],
        ),
        out_shape=[
            jax.ShapeDtypeStruct((trees, rows, width), BF16),
            jax.ShapeDtypeStruct((trees, rows // parts, width), BF16),
            jax.ShapeDtypeStruct((trees, rows, width), BF16),
        ],
        cost_estimate=pl.CostEstimate(
            flops=10 * tokens.size, bytes_accessed=8 * tokens.size, transcendentals=0
        ),
        name="first_norm",
    )(quarter, chunk, tokens, cotangent, gain, shift)


def replace_kernel(pieces, trees, quarter, chunk, *refs):
    o_ref = refs[2 * trees]
    part = o_ref.shape[2] // pieces
    step = pl.program_id(0)
    for half in range(2):

        @pl.when((step >= pl.num_programs(0) // 2) == (half == 1))
        def _():
            for i in range(trees):
                for k in range(pieces):
                    there = pl.ds(pl.multiple_of(chunk[k] * part, part), part)
                    o_ref[i, :, there] = refs[2 * i + half][:, k * part : (k + 1) * part]


def replace(quarter, chunk, values):
    half_rows, width = values[0][0].shape
    trees, parts = len(values), quarter.shape[0]
    turn = parts // 2
    block = (half_rows // turn, width)
    first = pl.BlockSpec(block, lambda r, q, c: (jnp.minimum(r, turn - 1), 0))
    second = pl.BlockSpec(block, lambda r, q, c: (jnp.maximum(r - turn, 0), 0))
    flat = [half for value in values for half in value]
    return pl.pallas_call(
        partial(replace_kernel, chunk.shape[0], trees),
        grid_spec=pltpu.PrefetchScalarGridSpec(
            num_scalar_prefetch=2,
            grid=(parts,),
            in_specs=[first, second] * trees,
            out_specs=pl.BlockSpec((trees,) + block, lambda r, q, c: (0, q[r], 0)),
        ),
        out_shape=jax.ShapeDtypeStruct((trees, 2 * half_rows, width), values[0][0].dtype),
        cost_estimate=pl.CostEstimate(flops=0, bytes_accessed=4 * trees * half_rows * width, transcendentals=0),
        name="replace",
    )(quarter, chunk, *flat)


def per_device(
    sizes,
    tokens,
    tree_position,
    segment,
    parent_table,
    norm1_gain,
    norm1_shift,
    query_weight,
    query_bias,
    key_weight,
    value_weight,
    value_bias,
    out_weight,
    out_bias,
    norm2_gain,
    norm2_shift,
    up_weight,
    up_bias,
    down_weight,
    down_bias,
    cotangent,
):
    n_f, n_c, n_t = sizes["fsdp"], sizes["ctx"], sizes["tp"]
    f, c, t = (lax.axis_index(name) for name in ("fsdp", "ctx", "tp"))
    trees, rows, width = tokens.shape
    part = width // n_f
    local_width = query_weight.shape[1]
    heads = local_width // HD
    assert heads == n_c
    span = 3 * HD
    bits, order = hypercube(n_t)
    quarter_rows = rows // n_t

    def shift_f(v, k):
        return lax.ppermute(v, "fsdp", [(i, (i + k) % n_f) for i in range(n_f)])

    def shift_c(v, k):
        return lax.ppermute(v, "ctx", [(i, (i + k) % n_c) for i in range(n_c)])

    def flip_t(v, b):
        return lax.ppermute(v, "tp", [(i, i ^ (1 << b)) for i in range(n_t)])

    def after(v, *others):
        return lax.optimization_barrier((v,) + others)[0]

    def pieces_of(v):
        return [v] + [shift_f(v, -k) for k in range(1, n_f)]

    def sum_rows(v):
        for b in range(bits):
            half = v.shape[0] // 2
            come = flip_t(v[half:].astype(BF16), b)
            v = v[:half].astype(F32) + come.astype(F32)
        return v

    def all_rows(v):
        for b in reversed(range(bits)):
            v = jnp.concatenate([v, flip_t(v, b)], axis=0)
        return v

    def both_halves(v, axis=0):
        for b in reversed(range(1, bits)):
            v = jnp.concatenate([v, flip_t(v, b)], axis=axis)
        return v, flip_t(v, 0)

    both = jnp.concatenate(
        [up_weight[:, k * part : (k + 1) * part] for k in range(up_weight.shape[1] // part)] + [down_weight], axis=0
    )
    every = lax.all_gather(both, "fsdp")

    quarter = jnp.stack([t ^ r for r in order]).astype(jnp.int32)
    chunk = jnp.stack([(f + k) % n_f for k in range(n_f)]).astype(jnp.int32)

    def roll_in(v):
        return jnp.concatenate(
            [lax.dynamic_slice_in_dim(v, chunk[k] * part, part, axis=-1) for k in range(n_f)], axis=-1
        )

    vectors = roll_in(
        jnp.stack([norm1_gain, norm1_shift, norm2_gain, norm2_shift, out_bias, down_bias])
    )
    gain1, shift1, gain2, shift2, bias_out, bias_down = (vectors[i : i + 1] for i in range(6))

    def my_head(q, k, v):
        return jnp.concatenate(
            [lax.dynamic_slice_in_dim(a, c * HD, HD, axis=1) for a in (q, k, v)], axis=1
        )

    def by_head(q, k, v):
        stacked = jnp.stack([a.reshape(a.shape[0], heads, HD) for a in (q, k, v)], axis=2)
        doubled = jnp.concatenate([stacked, stacked], axis=1)
        turned = lax.dynamic_slice_in_dim(doubled, c, heads, axis=1)
        return turned.reshape(q.shape[0], heads * span)

    w_own = pieces_of(my_head(query_weight, key_weight, value_weight))
    w_out = jnp.concatenate([out_weight, out_weight], axis=0)
    w_out = pieces_of(lax.dynamic_slice_in_dim(w_out, c * HD, local_width, axis=0))
    units = up_weight.shape[1]
    w_up, w_down = [up_weight], [down_weight]
    for k in range(1, n_f):
        other = lax.dynamic_index_in_dim(every, chunk[k], 0, keepdims=False)
        w_up.append(jnp.concatenate([other[j * part : (j + 1) * part] for j in range(units // part)], axis=1))
        w_down.append(other[units:])
    bias_own = my_head(query_bias[None], jnp.zeros_like(query_bias)[None], value_bias[None])

    n_seg = parent_table.shape[1]

    def relative(v):
        blocks = v.reshape(trees, n_t, quarter_rows)
        return jnp.concatenate(
            [lax.dynamic_slice_in_dim(blocks, quarter[r], 1, axis=1) for r in range(n_t)], axis=1
        ).reshape(trees, rows)

    places = relative(tree_position)[:, ::RUN] // RUN
    ahead = jnp.sum(
        (segment[:, None, :] < jnp.arange(n_seg, dtype=jnp.int32)[None, :, None]).astype(jnp.int32), axis=2
    )
    info = jnp.concatenate([places, ahead], axis=1)
    infos = [info] + [shift_c(info, k) for k in range(1, n_c)]

    tokens = after(tokens, both, *infos)
    normed0, inputs0, dy0 = first_norm(
        quarter[:1], chunk, tokens, cotangent, gain1, shift1, quarter_rows
    )
    rings = []
    for i in range(trees):
        ring = [normed0[i] if i == 0 else after(normed0[i], rings[-1][-1])]
        for k in range(1, n_c):
            ring.append(shift_c(ring[-1], 1))
        rings.append(ring)
    normed, _, dy = first_norm(quarter, chunk, after(tokens, normed0), cotangent, gain1, shift1, quarter_rows)
    infos = lax.optimization_barrier((*infos, normed))[:n_c]
    normed = after(normed, rings[0][min(2, n_c - 1)], *w_own[1:])

    runs = places.shape[1]
    place = jnp.concatenate([v[:, :runs] for v in infos], axis=1)
    starts = sum(v[:, runs:] for v in infos)
    tables = tree_tables(place, starts, parent_table, n_c * rows)

    def cols(v, k):
        return v[:, k * part : (k + 1) * part]

    def times(v, pieces):
        return sum(nn(cols(v, k), pieces[k]) for k in range(n_f))

    def times_back(v, pieces):
        return sum(nt(cols(v, k), pieces[k]) for k in range(n_f))

    def wide(v, pieces):
        return jnp.concatenate([nn(v, p) for p in pieces], axis=1)

    def wide_back(v, pieces):
        return jnp.concatenate([nt(v, p) for p in pieces], axis=1)

    def to_heads(v, width_each):
        return [v[:, :width_each]] + [
            shift_c(v[:, k * width_each : (k + 1) * width_each], k) for k in range(1, n_c)
        ]

    def from_heads(parts):
        return [parts[0]] + [shift_c(parts[k], -k) for k in range(1, n_c)]

    far = [[both_halves(ring[k]) for k in range(1, n_c)] for ring in rings]
    w_qkv = [by_head(query_weight, key_weight, value_weight)]
    w_far = [lax.all_gather(after(v, ring[-1]), "ctx") for v in w_own[1:]]

    kept = []
    for i in range(trees):
        table = tuple(v[i : i + 1] for v in tables)
        everyone = lax.pad(normed[i], jnp.zeros((), BF16), ((0, (n_c - 1) * rows, 0), (0, 0, 0)))
        for k in range(1, n_c):
            for r, half in enumerate(far[i][k - 1]):
                everyone = lax.dynamic_update_slice(everyone, half, (k * rows + r * (rows // 2), 0))
        qkv = (times(everyone, w_own) + bias_own).astype(BF16)[None]
        *attended_parts, lse = attention_fwd(table, n_c, qkv)
        attended = jnp.concatenate(from_heads([v[0] for v in attended_parts]), axis=1)
        x0 = inputs0[i].astype(F32)
        middle = x0 + sum_rows(wide(attended, w_out)) + bias_out
        mean = jnp.mean(middle, axis=1, keepdims=True)
        spread = jnp.mean((middle - mean) * (middle - mean), axis=1, keepdims=True)
        rstd = lax.rsqrt(spread + EPS)
        unit = (middle - mean) * rstd
        normed_mid = (unit * gain2 + shift2).astype(BF16)
        if i == 0:
            normed_mid = after(normed_mid, w_qkv[0])
        normed_mid = all_rows(normed_mid)
        kept.append((table, qkv, attended_parts, lse, attended, x0, middle, unit, rstd, normed_mid, everyone))

    for v in w_far:
        w_qkv.append(
            jnp.concatenate(
                [lax.dynamic_index_in_dim(v, (c + j) % n_c, 0, keepdims=False) for j in range(n_c)], axis=1
            )
        )

    inner = []
    for i in range(trees):
        normed_mid = kept[i][9]
        hidden = times(normed_mid, w_up) + up_bias[None]
        cdf = 0.5 * (1.0 + lax.erf(hidden * math.sqrt(0.5)))
        slope = cdf + hidden * (jnp.exp(-0.5 * hidden * hidden) * (1.0 / math.sqrt(2.0 * math.pi)))
        active = (hidden * cdf).astype(BF16)
        grad_hidden = (times_back(dy[i], w_down) * slope).astype(BF16)
        inner.append((active, grad_hidden, wide_back(grad_hidden, w_up)))

    dys = dy.reshape(trees * rows, width)
    down_product = [tn(jnp.concatenate([v[0] for v in inner], axis=0), cols(dys, k)) for k in range(n_f)]
    down_product[1:] = [v.astype(BF16) for v in down_product[1:]]

    back = []
    for i in range(trees):
        x0, middle, unit, rstd, normed_mid = kept[i][5:10]
        active, grad_hidden, grad_mid = inner[i]
        grad_mid = sum_rows(grad_mid)
        g = grad_mid * gain2
        moved = rstd * (
            g - jnp.mean(g, axis=1, keepdims=True) - unit * jnp.mean(g * unit, axis=1, keepdims=True)
        )
        grad_middle = dy[i, :quarter_rows].astype(F32) + moved
        branch0 = grad_middle.astype(BF16)
        if i == 0:
            branch0 = after(branch0, *down_product[1:])
        branch = all_rows(branch0)
        back.append(
            dict(
                active=active,
                grad_hidden=grad_hidden,
                normed_mid=normed_mid,
                attended=kept[i][4],
                branch=branch,
                branch0=branch0,
                grad_middle=grad_middle,
                gain2=jnp.sum(grad_mid * unit, axis=0),
                shift2=jnp.sum(grad_mid, axis=0),
                out_bias=jnp.sum(branch0.astype(F32), axis=0),
                down_bias=jnp.sum(dy[i, :quarter_rows].astype(F32), axis=0),
                up_bias=jnp.sum(grad_hidden.astype(F32), axis=0),
            )
        )

    def whole(name):
        return jnp.concatenate([b[name] for b in back], axis=0)

    def in_order(v):
        return jnp.concatenate(
            [lax.dynamic_slice_in_dim(v, ((n_f + k - f) % n_f) * part, part, axis=1) for k in range(n_f)], axis=1
        )

    def sent(parts):
        return [parts[0]] + [shift_f(parts[k].astype(BF16), k) for k in range(1, n_f)]

    def joined(parts, *others):
        total = parts[0].astype(F32)
        for k in range(1, n_f):
            total = total + after(parts[k], *others).astype(F32)
        return total.astype(BF16)

    def scatter(v, axis):
        return lax.psum_scatter(v, "ctx", scatter_dimension=axis, tiled=True).astype(F32)

    grad_hidden, normed_mid = whole("grad_hidden"), whole("normed_mid")
    part_down = sent(down_product)
    part_up = sent([tn(cols(normed_mid, k), grad_hidden) for k in range(n_f)])

    grad_attended = jnp.stack([times_back(b["branch"], w_out).astype(BF16) for b in back])
    grad_parts = [grad_attended[:, :, :HD]] + [
        shift_c(grad_attended[:, :, k * HD : (k + 1) * HD], k) for k in range(1, n_c)
    ]
    grad_parts = [[v[i : i + 1] for v in grad_parts] for i in range(trees)]

    heads_back = []
    own_back = []
    for i in range(trees):
        table, qkv, attended_parts, lse = kept[i][:4]
        if i == 0:
            total_down = joined(part_down, *[v for parts in grad_parts for v in parts])
            g_down = scatter(total_down, 1)
            ahead = [total_down, *w_far]
        else:
            ahead = heads_back[0] + [sums]
        *back_parts, own = attention_bwd(table, after(qkv, *ahead), attended_parts, grad_parts[i], lse)
        own_back.append(own[0])
        heads_back.append(from_heads([own[0, :rows]] + [v[0] for v in back_parts]))
        if i == 0:
            partial_sums = [
                wide(after(b["active"], own_back[0]), w_down).reshape(n_t, quarter_rows, width) for b in back
            ]
            sums = sum_rows(jnp.concatenate(partial_sums, axis=1)).reshape(trees, quarter_rows, width)
    results = both_halves(
        jnp.stack([kept[i][6] + sums[i] + bias_down for i in range(trees)]).astype(BF16), 1
    )
    results = [[half[i] for half in results] for i in range(trees)]

    total_up = joined(part_up, own_back[-1])
    g_up = scatter(after(total_up, g_down), 0)

    attended = after(whole("attended"), own_back[-1])
    attended = lax.dynamic_slice_in_dim(
        jnp.concatenate([attended, attended], axis=1), ((n_c - c) % n_c) * HD, local_width, axis=1
    )
    branch = after(whole("branch"), own_back[-1])
    part_out = sent([tn(attended, cols(branch, k)) for k in range(n_f)])
    own_back = [after(v, *(w for h in heads_back for w in h)) for v in own_back]
    part_own = sent([sum(tn(cols(kept[i][10], k), own_back[i]) for i in range(trees)) for k in range(n_f)])
    own_total = joined(part_own, total_up)
    share = part // n_c

    def own_rows(k):
        return lax.dynamic_slice_in_dim(own_total, ((c + k) % n_c) * share, share, axis=0)

    grads = []
    for i in range(trees):
        x0, grad_middle = kept[i][5], back[i]["grad_middle"]
        g = sum_rows(wide_back(jnp.concatenate(heads_back[i], axis=1), w_qkv))
        mean = jnp.mean(x0, axis=1, keepdims=True)
        spread = jnp.mean((x0 - mean) * (x0 - mean), axis=1, keepdims=True)
        rstd = lax.rsqrt(spread + EPS)
        unit = (x0 - mean) * rstd
        back[i]["gain1"] = jnp.sum(g * unit, axis=0)
        back[i]["shift1"] = jnp.sum(g, axis=0)
        g = g * gain1
        moved = rstd * (
            g - jnp.mean(g, axis=1, keepdims=True) - unit * jnp.mean(g * unit, axis=1, keepdims=True)
        )
        grads.append(both_halves((grad_middle + moved).astype(BF16)))

    come = [own_rows(0)] + [shift_c(own_rows(k), k) for k in range(1, n_c)]

    def by_source(parts):
        turned = jnp.stack([parts[(n_c - k) % n_c] for k in range(n_c)] * 2)
        return lax.dynamic_slice_in_dim(turned, (n_c - c) % n_c, n_c, axis=0)

    come = list(lax.optimization_barrier((*come, *[half for v in grads for half in v])))[:n_c]
    come = by_source(come).astype(F32)
    g_query, g_key, g_value = (
        jnp.concatenate([come[h, :, k * HD : (k + 1) * HD] for h in range(heads)], axis=1) for k in range(3)
    )

    g_out = scatter(after(joined(part_out, back[-1]["shift1"]), g_up), 1)

    names = ("gain1", "shift1", "out_bias", "gain2", "shift2", "down_bias")
    rolled = jnp.stack([sum(b[name] for b in back) for name in names])
    for b in range(bits):
        rolled = rolled + flip_t(rolled, b)
    mine_f = cols(rolled, 0)
    for k in range(1, n_f):
        mine_f = mine_f + shift_f(cols(rolled, k), k)

    def own_share(k):
        return lax.dynamic_slice_in_dim(mine_f, ((c + k) % n_c) * share, share, axis=1)

    own = own_share(0)
    for k in range(1, n_c):
        own = own + shift_c(own_share(k), k)

    head_sum = sum(jnp.sum(v.astype(F32), axis=0) for v in own_back)
    head_sum = after(head_sum, grads[-1][0])
    unit_sum = sum(b["up_bias"] for b in back)
    sums = jnp.concatenate([head_sum, unit_sum], axis=0)[None]
    for k in range(1, n_f):
        sums = sums + shift_f(jnp.concatenate([head_sum, unit_sum], axis=0)[None], k)
    all_sums = [sums] + [shift_c(sums, k) for k in range(1, n_c)]
    g_up_bias = sum(v[0, span:] for v in all_sums)
    by_head_sum = by_source([v[0, :span] for v in all_sums])
    return (
        replace(quarter, chunk, results),
        replace(quarter, chunk, grads),
        own[0],
        own[1],
        g_query,
        by_head_sum[:, :HD].reshape(local_width),
        g_key,
        g_value,
        by_head_sum[:, 2 * HD :].reshape(local_width),
        g_out,
        own[2],
        own[3],
        own[4],
        g_up,
        g_up_bias,
        g_down,
        own[5],
    )


def solution(mesh):
    in_specs = (
        P("fsdp", "ctx", None),
        P("fsdp", "ctx"),
        P("fsdp", "ctx"),
        P("fsdp", None),
        P(),
        P(),
        P("fsdp", "tp"),
        P("tp"),
        P("fsdp", "tp"),
        P("fsdp", "tp"),
        P("tp"),
        P("tp", "fsdp"),
        P(),
        P(),
        P(),
        P("fsdp", "tp"),
        P("tp"),
        P("tp", "fsdp"),
        P(),
        P("fsdp", "ctx", None),
    )
    out_specs = (
        P("fsdp", "ctx", None),
        P("fsdp", "ctx", None),
        P(("fsdp", "ctx")),
        P(("fsdp", "ctx")),
        P(("fsdp", "ctx"), "tp"),
        P("tp"),
        P(("fsdp", "ctx"), "tp"),
        P(("fsdp", "ctx"), "tp"),
        P("tp"),
        P("tp", ("fsdp", "ctx")),
        P(("fsdp", "ctx")),
        P(("fsdp", "ctx")),
        P(("fsdp", "ctx")),
        P(("fsdp", "ctx"), "tp"),
        P("tp"),
        P("tp", ("fsdp", "ctx")),
        P(("fsdp", "ctx")),
    )
    return jax.shard_map(
        partial(per_device, dict(mesh.shape)), mesh=mesh, in_specs=in_specs, out_specs=out_specs, check_vma=False
    )
```

```python
import math
from functools import partial

import jax
import jax.numpy as jnp
from jax import lax
from jax.experimental import pallas as pl
from jax.experimental.pallas import tpu as pltpu
from jax.sharding import PartitionSpec as P

HD = 128
RUN = 64
TILE = 256
SCALE = 1.0 / math.sqrt(HD)
SCALE2 = SCALE * math.log2(math.e)
NEG = -1e30
EPS = 1e-05
F32 = jnp.float32
BF16 = jnp.bfloat16


def nn(a, b):
    return lax.dot_general(a, b, (((1,), (0,)), ((), ())), preferred_element_type=F32)


def nt(a, b):
    return lax.dot_general(a, b, (((1,), (1,)), ((), ())), preferred_element_type=F32)


def tn(a, b):
    return lax.dot_general(a, b, (((0,), (0,)), ((), ())), preferred_element_type=F32)


def seg_of(pos,starts_ref,t,nseg):
    s=jnp.zeros_like(pos)
    for i in range(1,nseg): s=s+(pos>=starts_ref[t,i]).astype(jnp.int32)
    return s
def path_of(seg,path_ref,t,nseg):
    p=jnp.zeros_like(seg)
    for i in range(nseg): p=jnp.where(seg==i,path_ref[t,i],p)
    return p

def fwd_kernel(nsrc,place,starts,path,code,*refs):
    qkv_ref=refs[0]; outs=refs[1:nsrc+1]; lse_ref=refs[nsrc+1]
    qs,ks,vs,os,kbit,qpath,m_s,l_s,acc_s=refs[nsrc+2:]
    t=pl.program_id(0)
    rows=qkv_ref.shape[1]; local=rows//nsrc; per=local//RUN; n=rows//TILE
    nseg=path.shape[1]
    for s in range(nsrc):
        for j in range(per):
            d=pl.multiple_of(place[t,s*per+j]*RUN,RUN)
            blk=qkv_ref[0,s*local+j*RUN:s*local+(j+1)*RUN,:]
            qs[pl.ds(d,RUN),:]=blk[:,0:HD]; ks[pl.ds(d,RUN),:]=blk[:,HD:2*HD]; vs[pl.ds(d,RUN),:]=blk[:,2*HD:]
    pos=lax.broadcasted_iota(jnp.int32,(rows,HD),0)
    kbit[...]=jnp.left_shift(1,seg_of(pos,starts,t,nseg))
    qpos=lax.broadcasted_iota(jnp.int32,(n,TILE),0)*TILE+lax.broadcasted_iota(jnp.int32,(n,TILE),1)
    qpath[...]=path_of(seg_of(qpos,starts,t,nseg),path,t,nseg)
    def qloop(qi,_):
        q0=pl.multiple_of(qi*TILE,TILE)
        m_s[...]=jnp.full_like(m_s,NEG); l_s[...]=jnp.zeros_like(l_s); acc_s[...]=jnp.zeros_like(acc_s)
        qt=qs[pl.ds(q0,TILE),:]
        qp=qpath[pl.ds(qi,1),:]
        def kloop(ki,_):
            k0=pl.multiple_of(ki*TILE,TILE)
            c=code[t,qi*n+ki]
            def step(masked):
                sT=nt(ks[pl.ds(k0,TILE),:],qt)
                if masked:
                    kb=kbit[pl.ds(k0,TILE),:]
                    kb=jnp.concatenate([kb]*(TILE//HD),axis=1)
                    diff=(q0-k0)+lax.broadcasted_iota(jnp.int32,(TILE,TILE),1)-lax.broadcasted_iota(jnp.int32,(TILE,TILE),0)
                    vis=((kb&qp)!=0)&(diff>=0)
                    sT=jnp.where(vis,sT,NEG)
                m0=m_s[...]
                m1=jnp.maximum(m0,jnp.max(sT,axis=0,keepdims=True))
                pT=jnp.exp2((sT-m1)*SCALE2)
                al=jnp.exp2((m0-m1)*SCALE2)
                l_s[...]=l_s[...]*al+jnp.sum(pT,axis=0,keepdims=True)
                acc_s[...]=acc_s[...]*al+tn(vs[pl.ds(k0,TILE),:],pT.astype(BF16))
                m_s[...]=m1
            @pl.when(c==2)
            def _(): step(False)
            @pl.when(c==1)
            def _(): step(True)
            return 0
        lax.fori_loop(0,qi+1,kloop,0)
        l=l_s[...]
        os[pl.ds(q0,TILE),:]=jnp.transpose(acc_s[...]/l).astype(BF16)
        lse_ref[0,pl.ds(qi,1),:]=m_s[...]*SCALE2+jnp.log2(l)
        return 0
    lax.fori_loop(0,n,qloop,0)
    for s in range(nsrc):
        for j in range(per):
            d=pl.multiple_of(place[t,s*per+j]*RUN,RUN)
            outs[s][0,j*RUN:(j+1)*RUN,:]=os[pl.ds(d,RUN),:]

def attention_fwd(tables,nsrc,qkv):
    place,starts,path,code=tables
    T,rows,_=qkv.shape; local=rows//nsrc; n=rows//TILE
    bs=lambda w: pl.BlockSpec((1,local,w),lambda t,*_:(t,0,0))
    return pl.pallas_call(partial(fwd_kernel,nsrc),
        grid_spec=pltpu.PrefetchScalarGridSpec(num_scalar_prefetch=4,grid=(T,),
            in_specs=[pl.BlockSpec((1,rows,3*HD),lambda t,*_:(t,0,0))],
            out_specs=[bs(HD)]*nsrc+[pl.BlockSpec((1,n,TILE),lambda t,*_:(t,0,0))],
            scratch_shapes=[pltpu.VMEM((rows,HD),BF16)]*4+[pltpu.VMEM((rows,HD),jnp.int32),pltpu.VMEM((n,TILE),jnp.int32),
               pltpu.VMEM((1,TILE),F32),pltpu.VMEM((1,TILE),F32),pltpu.VMEM((HD,TILE),F32)]),
        out_shape=[jax.ShapeDtypeStruct((T,local,HD),BF16)]*nsrc+[jax.ShapeDtypeStruct((T,n,TILE),F32)],
        cost_estimate=pl.CostEstimate(flops=T*rows*rows*HD*20,bytes_accessed=T*rows*HD*8,transcendentals=T*rows*rows//2),
        name="tree_attention")(place,starts,path,code,qkv)

def bwd_kernel(nsrc,place,starts,path,code,*refs):
    qkv_ref=refs[0]; oin=refs[1:nsrc+1]; gin=refs[nsrc+1:2*nsrc+1]; lse_ref=refs[2*nsrc+1]
    outs=refs[2*nsrc+2:3*nsrc+1]; whole_ref=refs[3*nsrc+1]
    qs,ks,vs,gs,os,kbit,qpath,dsum,dq,dk,dv,sorted_out=refs[3*nsrc+2:]
    t=pl.program_id(0)
    rows=qkv_ref.shape[1]; local=rows//nsrc; per=local//RUN; n=rows//TILE
    nseg=path.shape[1]
    for s in range(nsrc):
        for j in range(per):
            d=pl.multiple_of(place[t,s*per+j]*RUN,RUN)
            blk=qkv_ref[0,s*local+j*RUN:s*local+(j+1)*RUN,:]
            qs[pl.ds(d,RUN),:]=blk[:,0:HD]; ks[pl.ds(d,RUN),:]=blk[:,HD:2*HD]; vs[pl.ds(d,RUN),:]=blk[:,2*HD:]
            gs[pl.ds(d,RUN),:]=gin[s][0,j*RUN:(j+1)*RUN,:]; os[pl.ds(d,RUN),:]=oin[s][0,j*RUN:(j+1)*RUN,:]
    pos=lax.broadcasted_iota(jnp.int32,(rows,HD),0)
    kbit[...]=jnp.left_shift(1,seg_of(pos,starts,t,nseg))
    qpos=lax.broadcasted_iota(jnp.int32,(n,TILE),0)*TILE+lax.broadcasted_iota(jnp.int32,(n,TILE),1)
    qpath[...]=path_of(seg_of(qpos,starts,t,nseg),path,t,nseg)
    def dloop(qi,_):
        q0=pl.multiple_of(qi*TILE,TILE)
        prod=gs[pl.ds(q0,TILE),:].astype(F32)*os[pl.ds(q0,TILE),:].astype(F32)
        dsum[pl.ds(qi,1),:]=jnp.sum(jnp.transpose(prod),axis=0,keepdims=True)
        return 0
    lax.fori_loop(0,n,dloop,0)
    dq[...]=jnp.zeros_like(dq)
    def kloop(ki,_):
        k0=pl.multiple_of(ki*TILE,TILE)
        kt=ks[pl.ds(k0,TILE),:]; vt=vs[pl.ds(k0,TILE),:]
        dk[...]=jnp.zeros_like(dk); dv[...]=jnp.zeros_like(dv)
        def qloop(qi,_):
            q0=pl.multiple_of(qi*TILE,TILE)
            c=code[t,qi*n+ki]
            def step(masked):
                qt=qs[pl.ds(q0,TILE),:]; gt=gs[pl.ds(q0,TILE),:]
                sT=nt(kt,qt)
                dpT=nt(vt,gt)
                pT=jnp.exp2(sT*SCALE2-lse_ref[0,pl.ds(qi,1),:])
                if masked:
                    kb=kbit[pl.ds(k0,TILE),:]
                    kb=jnp.concatenate([kb]*(TILE//HD),axis=1)
                    qp=qpath[pl.ds(qi,1),:]
                    diff=(q0-k0)+lax.broadcasted_iota(jnp.int32,(TILE,TILE),1)-lax.broadcasted_iota(jnp.int32,(TILE,TILE),0)
                    vis=((kb&qp)!=0)&(diff>=0)
                    pT=jnp.where(vis,pT,0.0)
                dsT=(pT*(dpT-dsum[pl.ds(qi,1),:])).astype(BF16)
                dv[...]+=nn(pT.astype(BF16),gt)
                dk[...]+=nn(dsT,qt)
                dq[pl.ds(q0,TILE),:]+=tn(dsT,kt)
            @pl.when(c==2)
            def _(): step(False)
            @pl.when(c==1)
            def _(): step(True)
            return 0
        lax.fori_loop(ki,n,qloop,0)
        sorted_out[pl.ds(k0,TILE),HD:2*HD]=(dk[...]*SCALE).astype(BF16)
        sorted_out[pl.ds(k0,TILE),2*HD:]=dv[...].astype(BF16)
        return 0
    lax.fori_loop(0,n,kloop,0)
    sorted_out[:,0:HD]=(dq[...]*SCALE).astype(BF16)
    for s in range(nsrc):
        for j in range(per):
            d=pl.multiple_of(place[t,s*per+j]*RUN,RUN)
            blk=sorted_out[pl.ds(d,RUN),:]
            whole_ref[0,s*local+j*RUN:s*local+(j+1)*RUN,:]=blk
            if s: outs[s-1][0,j*RUN:(j+1)*RUN,:]=blk

def attention_bwd(tables,qkv,oparts,gparts,lse):
    place,starts,path,code=tables
    nsrc=len(oparts); T,rows,_=qkv.shape; local=rows//nsrc; n=rows//TILE
    bs=lambda w: pl.BlockSpec((1,local,w),lambda t,*_:(t,0,0))
    return pl.pallas_call(partial(bwd_kernel,nsrc),
        grid_spec=pltpu.PrefetchScalarGridSpec(num_scalar_prefetch=4,grid=(T,),
            in_specs=[pl.BlockSpec((1,rows,3*HD),lambda t,*_:(t,0,0))]+[bs(HD)]*(2*nsrc)+[pl.BlockSpec((1,n,TILE),lambda t,*_:(t,0,0))],
            out_specs=[bs(3*HD)]*(nsrc-1)+[pl.BlockSpec((1,rows,3*HD),lambda t,*_:(t,0,0))],
            scratch_shapes=[pltpu.VMEM((rows,HD),BF16)]*5+[pltpu.VMEM((rows,HD),jnp.int32),pltpu.VMEM((n,TILE),jnp.int32),
               pltpu.VMEM((n,TILE),F32),pltpu.VMEM((rows,HD),F32),pltpu.VMEM((TILE,HD),F32),pltpu.VMEM((TILE,HD),F32),
               pltpu.VMEM((rows,3*HD),BF16)]),
        out_shape=[jax.ShapeDtypeStruct((T,local,3*HD),BF16)]*(nsrc-1)+[jax.ShapeDtypeStruct((T,rows,3*HD),BF16)],
        cost_estimate=pl.CostEstimate(flops=T*rows*rows*HD*25,bytes_accessed=T*rows*HD*20,transcendentals=T*rows*rows//2),
        name="tree_attention_back")(place,starts,path,code,qkv,*oparts,*gparts,lse)


def tree_tables(place, starts, parent, rows):
    labels = jnp.arange(parent.shape[1], dtype=jnp.int32)
    second = jnp.sum(jnp.where(parent[:, :, None] == labels, parent[:, None, :], 0), axis=2)
    path = (1 << labels)[None] | (1 << parent) | (1 << second)
    tiles = rows // TILE
    first_row = jnp.arange(tiles, dtype=jnp.int32)[None, :, None] * TILE
    low = jnp.sum((first_row >= starts[:, None, :]).astype(jnp.int32), axis=2) - 1
    high = jnp.sum((first_row + TILE - 1 >= starts[:, None, :]).astype(jnp.int32), axis=2) - 1
    inside = (labels >= low[:, :, None]) & (labels <= high[:, :, None])
    see = ((path[:, :, None] >> labels) & 1) == 1
    pair = inside[:, :, None, :, None] & inside[:, None, :, None, :]
    some = jnp.any(pair & see[:, None, None], axis=(3, 4))
    every = jnp.all((~pair) | see[:, None, None], axis=(3, 4))
    query = jnp.arange(tiles)[:, None]
    key = jnp.arange(tiles)[None, :]
    code = jnp.where((key > query) | ~some, 0, jnp.where(every & (key < query), 2, 1))
    return (
        place.astype(jnp.int32),
        starts.astype(jnp.int32),
        path.astype(jnp.int32),
        code.astype(jnp.int32).reshape(-1, tiles * tiles),
    )


def hypercube(n):
    bits = n.bit_length() - 1
    order = [sum(((r >> b) & 1) << (bits - 1 - b) for b in range(bits)) for r in range(n)]
    return bits, order


def first_norm_kernel(pieces, quarter, chunk, x_ref, dy_ref, gain_ref, shift_ref, n_ref, x0_ref, dyr_ref):
    width = x_ref.shape[2]
    part = width // pieces
    x = x_ref[0].astype(F32)
    mean = jnp.mean(x, axis=1, keepdims=True)
    spread = jnp.mean((x - mean) * (x - mean), axis=1, keepdims=True)
    scale = lax.rsqrt(spread + EPS)
    for k in range(pieces):
        here = slice(k * part, (k + 1) * part)
        there = pl.ds(pl.multiple_of(chunk[k] * part, part), part)
        xk = x_ref[0, :, there]
        n_ref[0, :, here] = (
            (xk.astype(F32) - mean) * scale * gain_ref[:, here] + shift_ref[:, here]
        ).astype(BF16)
        dyr_ref[0, :, here] = dy_ref[0, :, there]

        @pl.when(pl.program_id(1) == 0)
        def _():
            x0_ref[0, :, here] = xk


def first_norm(quarter, chunk, tokens, cotangent, gain, shift, block_rows):
    trees, _, width = tokens.shape
    parts = quarter.shape[0]
    rows = parts * block_rows
    block = (1, block_rows, width)
    come = pl.BlockSpec(block, lambda i, r, q, c: (i, q[r], 0))
    go = pl.BlockSpec(block, lambda i, r, q, c: (i, r, 0))
    row = pl.BlockSpec((1, width), lambda i, r, q, c: (0, 0))
    return pl.pallas_call(
        partial(first_norm_kernel, chunk.shape[0]),
        grid_spec=pltpu.PrefetchScalarGridSpec(
            num_scalar_prefetch=2,
            grid=(trees, parts),
            in_specs=[come, come, row, row],
            out_specs=[go, pl.BlockSpec(block, lambda i, r, q, c: (i, 0, 0)), go],
        ),
        out_shape=[
            jax.ShapeDtypeStruct((trees, rows, width), BF16),
            jax.ShapeDtypeStruct((trees, rows // parts, width), BF16),
            jax.ShapeDtypeStruct((trees, rows, width), BF16),
        ],
        cost_estimate=pl.CostEstimate(
            flops=10 * tokens.size, bytes_accessed=8 * tokens.size, transcendentals=0
        ),
        name="first_norm",
    )(quarter, chunk, tokens, cotangent, gain, shift)


def replace_kernel(pieces, trees, quarter, chunk, *refs):
    o_ref = refs[2 * trees]
    part = o_ref.shape[2] // pieces
    step = pl.program_id(0)
    for half in range(2):

        @pl.when((step >= pl.num_programs(0) // 2) == (half == 1))
        def _():
            for i in range(trees):
                for k in range(pieces):
                    there = pl.ds(pl.multiple_of(chunk[k] * part, part), part)
                    o_ref[i, :, there] = refs[2 * i + half][:, k * part : (k + 1) * part]


def replace(quarter, chunk, values):
    half_rows, width = values[0][0].shape
    trees, parts = len(values), quarter.shape[0]
    turn = parts // 2
    block = (half_rows // turn, width)
    first = pl.BlockSpec(block, lambda r, q, c: (jnp.minimum(r, turn - 1), 0))
    second = pl.BlockSpec(block, lambda r, q, c: (jnp.maximum(r - turn, 0), 0))
    flat = [half for value in values for half in value]
    return pl.pallas_call(
        partial(replace_kernel, chunk.shape[0], trees),
        grid_spec=pltpu.PrefetchScalarGridSpec(
            num_scalar_prefetch=2,
            grid=(parts,),
            in_specs=[first, second] * trees,
            out_specs=pl.BlockSpec((trees,) + block, lambda r, q, c: (0, q[r], 0)),
        ),
        out_shape=jax.ShapeDtypeStruct((trees, 2 * half_rows, width), values[0][0].dtype),
        cost_estimate=pl.CostEstimate(flops=0, bytes_accessed=4 * trees * half_rows * width, transcendentals=0),
        name="replace",
    )(quarter, chunk, *flat)


def per_device(
    sizes,
    tokens,
    tree_position,
    segment,
    parent_table,
    norm1_gain,
    norm1_shift,
    query_weight,
    query_bias,
    key_weight,
    value_weight,
    value_bias,
    out_weight,
    out_bias,
    norm2_gain,
    norm2_shift,
    up_weight,
    up_bias,
    down_weight,
    down_bias,
    cotangent,
):
    n_f, n_c, n_t = sizes["fsdp"], sizes["ctx"], sizes["tp"]
    f, c, t = (lax.axis_index(name) for name in ("fsdp", "ctx", "tp"))
    trees, rows, width = tokens.shape
    part = width // n_f
    local_width = query_weight.shape[1]
    heads = local_width // HD
    assert heads == n_c
    span = 3 * HD
    bits, order = hypercube(n_t)
    quarter_rows = rows // n_t

    def shift_f(v, k):
        return lax.ppermute(v, "fsdp", [(i, (i + k) % n_f) for i in range(n_f)])

    def shift_c(v, k):
        return lax.ppermute(v, "ctx", [(i, (i + k) % n_c) for i in range(n_c)])

    def flip_t(v, b):
        return lax.ppermute(v, "tp", [(i, i ^ (1 << b)) for i in range(n_t)])

    def after(v, *others):
        return lax.optimization_barrier((v,) + others)[0]

    def pieces_of(v):
        return [v] + [shift_f(v, -k) for k in range(1, n_f)]

    def sum_rows(v, first=0, last=bits):
        for b in range(first, last):
            half = v.shape[0] // 2
            come = flip_t(v[half:].astype(BF16), b)
            v = v[:half].astype(F32) + come.astype(F32)
        return v

    def all_rows(v):
        for b in reversed(range(bits)):
            v = jnp.concatenate([v, flip_t(v, b)], axis=0)
        return v

    def both_halves(v, axis=0):
        for b in reversed(range(1, bits)):
            v = jnp.concatenate([v, flip_t(v, b)], axis=axis)
        return v, flip_t(v, 0)

    both = jnp.concatenate(
        [up_weight[:, k * part : (k + 1) * part] for k in range(up_weight.shape[1] // part)] + [down_weight], axis=0
    )
    every = lax.all_gather(both, "fsdp")

    quarter = jnp.stack([t ^ r for r in order]).astype(jnp.int32)
    chunk = jnp.stack([(f + k) % n_f for k in range(n_f)]).astype(jnp.int32)

    def roll_in(v):
        return jnp.concatenate(
            [lax.dynamic_slice_in_dim(v, chunk[k] * part, part, axis=-1) for k in range(n_f)], axis=-1
        )

    vectors = roll_in(
        jnp.stack([norm1_gain, norm1_shift, norm2_gain, norm2_shift, out_bias, down_bias])
    )
    gain1, shift1, gain2, shift2, bias_out, bias_down = (vectors[i : i + 1] for i in range(6))

    def my_head(q, k, v):
        return jnp.concatenate(
            [lax.dynamic_slice_in_dim(a, c * HD, HD, axis=1) for a in (q, k, v)], axis=1
        )

    def by_head(q, k, v):
        stacked = jnp.stack([a.reshape(a.shape[0], heads, HD) for a in (q, k, v)], axis=2)
        doubled = jnp.concatenate([stacked, stacked], axis=1)
        turned = lax.dynamic_slice_in_dim(doubled, c, heads, axis=1)
        return turned.reshape(q.shape[0], heads * span)

    w_own = pieces_of(my_head(query_weight, key_weight, value_weight))
    w_out = jnp.concatenate([out_weight, out_weight], axis=0)
    w_out = pieces_of(lax.dynamic_slice_in_dim(w_out, c * HD, local_width, axis=0))
    units = up_weight.shape[1]
    w_up, w_down = [up_weight], [down_weight]
    for k in range(1, n_f):
        other = lax.dynamic_index_in_dim(every, chunk[k], 0, keepdims=False)
        w_up.append(jnp.concatenate([other[j * part : (j + 1) * part] for j in range(units // part)], axis=1))
        w_down.append(other[units:])
    bias_own = my_head(query_bias[None], jnp.zeros_like(query_bias)[None], value_bias[None])

    n_seg = parent_table.shape[1]

    def relative(v):
        blocks = v.reshape(trees, n_t, quarter_rows)
        return jnp.concatenate(
            [lax.dynamic_slice_in_dim(blocks, quarter[r], 1, axis=1) for r in range(n_t)], axis=1
        ).reshape(trees, rows)

    places = relative(tree_position)[:, ::RUN] // RUN
    ahead = jnp.sum(
        (segment[:, None, :] < jnp.arange(n_seg, dtype=jnp.int32)[None, :, None]).astype(jnp.int32), axis=2
    )
    info = jnp.concatenate([places, ahead], axis=1)
    infos = [info] + [shift_c(info, k) for k in range(1, n_c)]

    tokens = after(tokens, both, *infos)
    normed0, inputs0, dy0 = first_norm(
        quarter[:1], chunk, tokens, cotangent, gain1, shift1, quarter_rows
    )
    rings = []
    for i in range(trees):
        ring = [normed0[i] if i == 0 else after(normed0[i], rings[-1][-1])]
        for k in range(1, n_c):
            ring.append(shift_c(ring[-1], 1))
        rings.append(ring)
    normed, _, dy = first_norm(quarter, chunk, after(tokens, normed0), cotangent, gain1, shift1, quarter_rows)
    infos = lax.optimization_barrier((*infos, normed))[:n_c]
    normed = after(normed, rings[0][min(2, n_c - 1)], *w_own[1:])

    runs = places.shape[1]
    place = jnp.concatenate([v[:, :runs] for v in infos], axis=1)
    starts = sum(v[:, runs:] for v in infos)
    tables = tree_tables(place, starts, parent_table, n_c * rows)

    def cols(v, k):
        return v[:, k * part : (k + 1) * part]

    def times(v, pieces):
        return sum(nn(cols(v, k), pieces[k]) for k in range(n_f))

    def times_back(v, pieces):
        return sum(nt(cols(v, k), pieces[k]) for k in range(n_f))

    def wide(v, pieces):
        return jnp.concatenate([nn(v, p) for p in pieces], axis=1)

    def wide_back(v, pieces):
        return jnp.concatenate([nt(v, p) for p in pieces], axis=1)

    def to_heads(v, width_each):
        return [v[:, :width_each]] + [
            shift_c(v[:, k * width_each : (k + 1) * width_each], k) for k in range(1, n_c)
        ]

    def from_heads(parts):
        return [parts[0]] + [shift_c(parts[k], -k) for k in range(1, n_c)]

    far = [[both_halves(ring[k]) for k in range(1, n_c)] for ring in rings]
    w_qkv = [by_head(query_weight, key_weight, value_weight)]
    w_far = [lax.all_gather(after(v, ring[-1]), "ctx") for v in w_own[1:]]

    kept = []
    for i in range(trees):
        table = tuple(v[i : i + 1] for v in tables)
        everyone = lax.pad(normed[i], jnp.zeros((), BF16), ((0, (n_c - 1) * rows, 0), (0, 0, 0)))
        for k in range(1, n_c):
            for r, half in enumerate(far[i][k - 1]):
                everyone = lax.dynamic_update_slice(everyone, half, (k * rows + r * (rows // 2), 0))
        qkv = (times(everyone, w_own) + bias_own).astype(BF16)[None]
        if i:
            held = list(kept[-1])
            qkv, held[6] = lax.optimization_barrier((qkv, held[6]))
            kept[-1] = tuple(held)
        *attended_parts, lse = attention_fwd(table, n_c, qkv)
        attended = jnp.concatenate(from_heads([v[0] for v in attended_parts]), axis=1)
        x0 = inputs0[i].astype(F32)
        middle = x0 + sum_rows(wide(attended, w_out)) + bias_out
        mean = jnp.mean(middle, axis=1, keepdims=True)
        spread = jnp.mean((middle - mean) * (middle - mean), axis=1, keepdims=True)
        rstd = lax.rsqrt(spread + EPS)
        unit = (middle - mean) * rstd
        normed_mid = (unit * gain2 + shift2).astype(BF16)
        if i == 0:
            normed_mid = after(normed_mid, w_qkv[0])
        normed_mid = all_rows(normed_mid)
        kept.append((table, qkv, attended_parts, lse, attended, x0, middle, unit, rstd, normed_mid, everyone))

    for v in w_far:
        w_qkv.append(
            jnp.concatenate(
                [lax.dynamic_index_in_dim(v, (c + j) % n_c, 0, keepdims=False) for j in range(n_c)], axis=1
            )
        )

    inner = []
    for i in range(trees):
        normed_mid = kept[i][9]
        hidden = times(normed_mid, w_up) + up_bias[None]
        cdf = 0.5 * (1.0 + lax.erf(hidden * math.sqrt(0.5)))
        slope = cdf + hidden * (jnp.exp(-0.5 * hidden * hidden) * (1.0 / math.sqrt(2.0 * math.pi)))
        active = (hidden * cdf).astype(BF16)
        grad_hidden = (times_back(dy[i], w_down) * slope).astype(BF16)
        inner.append((active, grad_hidden, wide_back(grad_hidden, w_up)))

    dys = dy.reshape(trees * rows, width)
    down_product = [tn(jnp.concatenate([v[0] for v in inner], axis=0), cols(dys, k)) for k in range(n_f)]
    down_product[1:] = [v.astype(BF16) for v in down_product[1:]]

    back = []
    for i in range(trees):
        x0, middle, unit, rstd, normed_mid = kept[i][5:10]
        active, grad_hidden, grad_mid = inner[i]
        grad_mid = sum_rows(grad_mid)
        g = grad_mid * gain2
        moved = rstd * (
            g - jnp.mean(g, axis=1, keepdims=True) - unit * jnp.mean(g * unit, axis=1, keepdims=True)
        )
        grad_middle = dy[i, :quarter_rows].astype(F32) + moved
        branch0 = grad_middle.astype(BF16)
        if i == 0:
            branch0 = after(branch0, *down_product[1:])
        branch = all_rows(branch0)
        back.append(
            dict(
                active=active,
                grad_hidden=grad_hidden,
                normed_mid=normed_mid,
                attended=kept[i][4],
                branch=branch,
                branch0=branch0,
                grad_middle=grad_middle,
                gain2=jnp.sum(grad_mid * unit, axis=0),
                shift2=jnp.sum(grad_mid, axis=0),
                out_bias=jnp.sum(branch0.astype(F32), axis=0),
                down_bias=jnp.sum(dy[i, :quarter_rows].astype(F32), axis=0),
                up_bias=jnp.sum(grad_hidden.astype(F32), axis=0),
            )
        )

    def whole(name):
        return jnp.concatenate([b[name] for b in back], axis=0)

    def in_order(v):
        return jnp.concatenate(
            [lax.dynamic_slice_in_dim(v, ((n_f + k - f) % n_f) * part, part, axis=1) for k in range(n_f)], axis=1
        )

    def sent(parts):
        return [parts[0]] + [shift_f(parts[k].astype(BF16), k) for k in range(1, n_f)]

    def joined(parts, *others):
        total = parts[0].astype(F32)
        for k in range(1, n_f):
            total = total + after(parts[k], *others).astype(F32)
        return total.astype(BF16)

    def scatter(v, axis):
        return lax.psum_scatter(v, "ctx", scatter_dimension=axis, tiled=True).astype(F32)

    grad_hidden, normed_mid = whole("grad_hidden"), whole("normed_mid")
    part_down = sent(down_product)
    part_up = sent([tn(cols(normed_mid, k), grad_hidden) for k in range(n_f)])

    grad_attended = jnp.stack([times_back(b["branch"], w_out).astype(BF16) for b in back])
    grad_parts = [grad_attended[:, :, :HD]] + [
        shift_c(grad_attended[:, :, k * HD : (k + 1) * HD], k) for k in range(1, n_c)
    ]
    grad_parts = [[v[i : i + 1] for v in grad_parts] for i in range(trees)]

    heads_back = []
    own_back = []
    for i in range(trees):
        table, qkv, attended_parts, lse = kept[i][:4]
        if i == 0:
            total_down = joined(part_down, *[v for parts in grad_parts for v in parts])
            g_down = scatter(total_down, 1)
            ahead = [total_down, *w_far]
        else:
            ahead = heads_back[0]
        *back_parts, own = attention_bwd(table, after(qkv, *ahead), attended_parts, grad_parts[i], lse)
        own_back.append(own[0])
        heads_back.append(from_heads([own[0, :rows]] + [v[0] for v in back_parts]))
        if i == 0:
            partial_sums = [
                wide(after(b["active"], own_back[0]), w_down).reshape(n_t, quarter_rows, width) for b in back
            ]
            sums = sum_rows(jnp.concatenate(partial_sums, axis=1)).reshape(trees, quarter_rows, width)
    *heads_back[-1], sums, g_down = lax.optimization_barrier((*heads_back[-1], sums, g_down))
    results = both_halves(
        jnp.stack([kept[i][6] + sums[i] + bias_down for i in range(trees)]).astype(BF16), 1
    )
    results = [[half[i] for half in results] for i in range(trees)]

    total_up = joined(part_up, own_back[-1])
    g_up = scatter(after(total_up, g_down), 0)

    attended = after(whole("attended"), own_back[-1])
    attended = lax.dynamic_slice_in_dim(
        jnp.concatenate([attended, attended], axis=1), ((n_c - c) % n_c) * HD, local_width, axis=1
    )
    branch = after(whole("branch"), own_back[-1])
    part_out = sent([tn(attended, cols(branch, k)) for k in range(n_f)])
    own_back = [after(v, *(w for h in heads_back for w in h)) for v in own_back]
    part_own = sent([sum(tn(cols(kept[i][10], k), own_back[i]) for i in range(trees)) for k in range(n_f)])
    own_total = joined(part_own, total_up)
    share = part // n_c

    def own_rows(k):
        return lax.dynamic_slice_in_dim(own_total, ((c + k) % n_c) * share, share, axis=0)

    grads = []
    for i in range(trees):
        x0, grad_middle = kept[i][5], back[i]["grad_middle"]
        g = sum_rows(wide_back(jnp.concatenate(heads_back[i], axis=1), w_qkv), 0, bits - 1)
        if i == trees - 1:
            g, g_up = lax.optimization_barrier((g, g_up))
            g_out = scatter(after(joined(part_out, *heads_back[-1]), g_up), 1)
        g = sum_rows(g, bits - 1)
        mean = jnp.mean(x0, axis=1, keepdims=True)
        spread = jnp.mean((x0 - mean) * (x0 - mean), axis=1, keepdims=True)
        rstd = lax.rsqrt(spread + EPS)
        unit = (x0 - mean) * rstd
        back[i]["gain1"] = jnp.sum(g * unit, axis=0)
        back[i]["shift1"] = jnp.sum(g, axis=0)
        g = g * gain1
        moved = rstd * (
            g - jnp.mean(g, axis=1, keepdims=True) - unit * jnp.mean(g * unit, axis=1, keepdims=True)
        )
        moved = (grad_middle + moved).astype(BF16)
        if i == trees - 1:
            moved = after(moved, *[v[0] for v in results], grads[0][0])
            moved, g_out = lax.optimization_barrier((moved, g_out))
        grads.append(both_halves(moved))

    come = [own_rows(0)] + [shift_c(own_rows(k), k) for k in range(1, n_c)]

    def by_source(parts):
        turned = jnp.stack([parts[(n_c - k) % n_c] for k in range(n_c)] * 2)
        return lax.dynamic_slice_in_dim(turned, (n_c - c) % n_c, n_c, axis=0)

    come = list(lax.optimization_barrier((*come, moved)))[:n_c]
    come = by_source(come).astype(F32)
    g_query, g_key, g_value = (
        jnp.concatenate([come[h, :, k * HD : (k + 1) * HD] for h in range(heads)], axis=1) for k in range(3)
    )


    names = ("gain1", "shift1", "out_bias", "gain2", "shift2", "down_bias")
    rolled = jnp.stack([sum(b[name] for b in back) for name in names])
    for b in range(bits):
        rolled = rolled + flip_t(rolled, b)
    mine_f = cols(rolled, 0)
    for k in range(1, n_f):
        mine_f = mine_f + shift_f(cols(rolled, k), k)

    def own_share(k):
        return lax.dynamic_slice_in_dim(mine_f, ((c + k) % n_c) * share, share, axis=1)

    own = own_share(0)
    for k in range(1, n_c):
        own = own + shift_c(own_share(k), k)

    head_sum = sum(jnp.sum(v.astype(F32), axis=0) for v in own_back)
    head_sum = after(head_sum, grads[-1][0])
    unit_sum = sum(b["up_bias"] for b in back)
    sums = jnp.concatenate([head_sum, unit_sum], axis=0)[None]
    for k in range(1, n_f):
        sums = sums + shift_f(jnp.concatenate([head_sum, unit_sum], axis=0)[None], k)
    all_sums = [sums] + [shift_c(sums, k) for k in range(1, n_c)]
    g_up_bias = sum(v[0, span:] for v in all_sums)
    by_head_sum = by_source([v[0, :span] for v in all_sums])
    return (
        replace(quarter, chunk, results),
        replace(quarter, chunk, grads),
        own[0],
        own[1],
        g_query,
        by_head_sum[:, :HD].reshape(local_width),
        g_key,
        g_value,
        by_head_sum[:, 2 * HD :].reshape(local_width),
        g_out,
        own[2],
        own[3],
        own[4],
        g_up,
        g_up_bias,
        g_down,
        own[5],
    )


def solution(mesh):
    in_specs = (
        P("fsdp", "ctx", None),
        P("fsdp", "ctx"),
        P("fsdp", "ctx"),
        P("fsdp", None),
        P(),
        P(),
        P("fsdp", "tp"),
        P("tp"),
        P("fsdp", "tp"),
        P("fsdp", "tp"),
        P("tp"),
        P("tp", "fsdp"),
        P(),
        P(),
        P(),
        P("fsdp", "tp"),
        P("tp"),
        P("tp", "fsdp"),
        P(),
        P("fsdp", "ctx", None),
    )
    out_specs = (
        P("fsdp", "ctx", None),
        P("fsdp", "ctx", None),
        P(("fsdp", "ctx")),
        P(("fsdp", "ctx")),
        P(("fsdp", "ctx"), "tp"),
        P("tp"),
        P(("fsdp", "ctx"), "tp"),
        P(("fsdp", "ctx"), "tp"),
        P("tp"),
        P("tp", ("fsdp", "ctx")),
        P(("fsdp", "ctx")),
        P(("fsdp", "ctx")),
        P(("fsdp", "ctx")),
        P(("fsdp", "ctx"), "tp"),
        P("tp"),
        P("tp", ("fsdp", "ctx")),
        P(("fsdp", "ctx")),
    )
    return jax.shard_map(
        partial(per_device, dict(mesh.shape)), mesh=mesh, in_specs=in_specs, out_specs=out_specs, check_vma=False
    )
```
